512 devices in a mesh: dom: 64 (over x, y, core), head: 8 (over z).
Axes of the slice: x: 4, y: 8, z: 8, core: 2. Of those that a mesh axis runs over, the one named last changes fastest.
Arguments:
- node_feats: bfloat16 [262144, 256], P(('dom', 'head'))
- w_qkv: bfloat16 [3, 256, 256], replicated, may hold values from -0.375 to 0.375
- w_graph: bfloat16 [256, 256], replicated, may hold values from -0.375 to 0.375
- ln_gain: float32 [256], replicated, may hold values from 0.1 to 1.9
- out_grad: bfloat16 [262144, 256], P(('dom', 'head')), may hold values from -6 to 6
- part_counts: int32 [512], P(('dom', 'head')), may hold values from 128 to 512, as said below
- send_rows: int32 [512, 2, 64], P(('dom', 'head')), may hold values from 0 to 511, as said below
- neighbours: int32 [262144, 16], P(('dom', 'head')), may hold values from 0 to 639, as said below
- neighbour_counts: int32 [262144], P(('dom', 'head')), may hold values from 1 to 16
Outputs:
- node_out: bfloat16 [262144, 256], P(('dom', 'head'))
- qkv_grad: float32 [3, 256, 256], replicated
- graph_grad: float32 [256, 256], replicated
The draws below stay inside these ranges and needn't reach their ends.
Inputs may be any that keep to these rules, and one draw needn't show every extreme that they name: `part_counts`: some partition is full in every draw. `send_rows`: every index is below the sending partition's count. `neighbours`: an index below 512 names a live row of the node's own partition; 512 + j names row j received from the partition before, 576 + j row j from the one after; the first partition never names rows from before, the last never rows from after.
All inputs are finite; a program needn't handle non-finite values.
Results may differ from the reference program's by a relative error of at most 0.0005.
The reference program's roundings to bfloat16 on the way (of `agg`, `dgraph` and `dprojs`) count: a program that leaves them out, or rounds other values in their place, can miss the bound.
Values may be sent and summed in bfloat16 or wider, within the bound.
No kernel may reach another device: no remote copies, remote signals or barrier semaphores. Data moves between devices by JAX's collectives and lax.ppermute only.
A program may use at most 64 MiB of HBM per device.

```python
import math
import jax
import jax.numpy as jnp
from jax import lax

D = 256
HEADS = 8
DH = 32
ROWS = 512
DEG = 16
HALO = 64
NPARTS = 512
NODES = 262144


def count_law(key):
    base = jax.random.fold_in(key, 11)
    first, second = jax.random.split(base)
    counts = jax.random.randint(first, (NPARTS,), ROWS // 4, ROWS + 1)
    full = jax.random.randint(second, (), 0, NPARTS)
    counts = jnp.where(jnp.arange(NPARTS) == full, ROWS, counts).astype(jnp.int32)
    return (counts, full)


def draw_part_counts(key, part):
    return count_law(key)[0]


def draw_send_rows(key, part):
    counts, full = count_law(key)
    raw = jax.random.randint(jax.random.fold_in(key, 12), (NPARTS, 2, HALO), 0, 2 ** 30)
    chosen = raw % counts[:, None, None]
    chosen = chosen.at[full, 0, 0].set(ROWS - 1)
    chosen = chosen.at[full, 1, 0].set(0)
    return chosen.astype(jnp.int32)


def draw_neighbours(key, part):
    counts, full = count_law(key)
    owner = jnp.arange(NODES, dtype=jnp.int32) // ROWS
    raw = jax.random.randint(jax.random.fold_in(key, 13), (NODES, DEG), 0, 2 ** 30)
    remote_pick = jax.random.randint(jax.random.fold_in(key, 14), (NODES, DEG), 0, 10)
    side = jax.random.randint(jax.random.fold_in(key, 15), (NODES, DEG), 0, 2)
    side = jnp.where(owner[:, None] == 0, 1, jnp.where(owner[:, None] == NPARTS - 1, 0, side))
    local = raw % counts[owner][:, None]
    remote = ROWS + side * HALO + raw % HALO
    chosen = jnp.where(remote_pick < 3, remote, local)
    chosen = chosen.at[0, 0].set(0)
    chosen = chosen.at[0, DEG - 1].set(ROWS + 2 * HALO - 1)
    return chosen.astype(jnp.int32)


def draw_node_feats(key, part):
    first, second = jax.random.split(key, 2)
    owner = (jnp.arange(NODES) // ROWS).astype(jnp.float32)
    rising = jnp.exp(math.log(3.0) * owner / max(NPARTS - 1, 1))
    offset = 0.6 * jax.random.normal(second, (D,), jnp.float32)
    base = jax.random.normal(first, (NODES, D), jnp.float32)
    values = 0.6 * rising[:, None] * (base + offset[None, :])
    return values.astype(jnp.bfloat16)


def plant(values, key, low, top_value):
    shape = values.shape
    spot = [jax.random.randint(jax.random.fold_in(key, axis), (), 0, shape[axis]) for axis in range(len(shape))]
    values = values.at[tuple(spot)].set(low)
    longest = shape.index(max(shape))
    spot[longest] = (spot[longest] + 1) % shape[longest]
    return values.at[tuple(spot)].set(top_value)


def block_scale(own_key, extent, cuts, low, top_value):
    level, own = 1.0, jax.random.fold_in(own_key, 6)
    for axis_at, parts in cuts:
        draws = jnp.exp(jax.random.uniform(jax.random.fold_in(own, axis_at), (parts,), jnp.float32, low / len(cuts), top_value / len(cuts)))
        level = level * jnp.repeat(draws, extent[axis_at] // parts).reshape([-1 if axis == axis_at else 1 for axis in range(len(extent))])
    return level


def normal_values(rng, dims, scale, most, cuts=(), kind=jnp.bfloat16):
    drawn = jax.random.normal(rng, dims, jnp.float32) * scale
    if len(cuts) > 0:
        drawn = block_scale(rng, dims, cuts, -0.22, 0.18) * drawn
    return jnp.clip(drawn, min=-most, max=most).astype(kind)


def setup_inputs(seed: int = 0) -> dict:
    splits = jax.random.split(jax.random.key(seed), 10)
    return {
        "node_feats": draw_node_feats(jax.random.fold_in(splits[9], 71), 0),
        "w_qkv": normal_values(splits[1], (3, D, D), D ** -0.5, 0.375),
        "w_graph": normal_values(splits[2], (D, D), D ** -0.5, 0.375),
        "ln_gain": jnp.clip(1.0 + 0.18 * jax.random.normal(splits[3], (D,), jnp.float32), 0.1, 1.9),
        "out_grad": normal_values(splits[4], (NODES, D), 1.0, 6.0, ((0, 512),)),
        "part_counts": draw_part_counts(jax.random.fold_in(splits[9], 71), 0),
        "send_rows": draw_send_rows(jax.random.fold_in(splits[9], 71), 0),
        "neighbours": draw_neighbours(jax.random.fold_in(splits[9], 71), 0),
        "neighbour_counts": plant(jax.random.randint(splits[8], (NODES,), 1, DEG + 1), jax.random.fold_in(splits[8], 1), 1, DEG).astype(jnp.int32),
    }


highest = lax.Precision.HIGHEST

def feature_map(value):
    return jnp.where(value > 0, value + 1.0, jnp.exp(jnp.minimum(value, 0.0)))

def feature_slope(value):
    return jnp.where(value > 0, jnp.ones_like(value), jnp.exp(jnp.minimum(value, 0.0)))

def combine_rows(source, around_left, around_right, neighbours, neighbour_counts):
    total_rows = source.shape[0]
    width = source.shape[1]
    block = min(256, total_rows)
    extended = jnp.concatenate([source, around_left, around_right], axis=0)

    def one_block(pieces):
        nbr_block, count_block, own_block = pieces
        picked = extended[nbr_block].astype(jnp.float32)
        slots = jnp.arange(nbr_block.shape[1], dtype=jnp.int32)
        usable = slots[None, :] < count_block[:, None]
        summed = lax.optimization_barrier(jnp.sum(jnp.where(usable[:, :, None], picked, jnp.zeros_like(picked)), axis=1))
        total = own_block.astype(jnp.float32) + summed
        return (total / (1.0 + count_block.astype(jnp.float32))[:, None]).astype(jnp.bfloat16)
    result = lax.map(one_block, (neighbours.reshape(total_rows // block, block, -1), neighbour_counts.reshape(total_rows // block, block), source.reshape(total_rows // block, block, width)))
    return result.reshape(total_rows, width)

def project(features, w_qkv):
    queries = jnp.dot(features, w_qkv[0], preferred_element_type=jnp.float32)
    key_rows = jnp.dot(features, w_qkv[1], preferred_element_type=jnp.float32)
    value_rows = jnp.dot(features, w_qkv[2], preferred_element_type=jnp.float32)
    return (queries, key_rows, value_rows)

def heads_of(matrix):
    return matrix.reshape(ROWS, HEADS, DH)

def reference(node_feats, w_qkv, w_graph, ln_gain, out_grad, part_counts, send_rows, neighbours, neighbour_counts):
    feats = node_feats.reshape(NPARTS, ROWS, D)
    packs = jax.vmap(lambda block_rows, chosen: block_rows[chosen])(feats, send_rows)
    empty = jnp.zeros((1, HALO, D), node_feats.dtype)
    from_left = jnp.concatenate([empty, packs[:-1, 1]], axis=0)
    from_right = jnp.concatenate([packs[1:, 0], empty], axis=0)
    alive = (jnp.arange(ROWS, dtype=jnp.int32)[None, :] < part_counts[:, None]).astype(jnp.float32)
    total_live = jnp.sum(part_counts.astype(jnp.float32))
    factor = 1.0 / (DH * total_live)
    nbr_parts = neighbours.reshape(NPARTS, ROWS, DEG)
    count_parts = neighbour_counts.reshape(NPARTS, ROWS)
    grad_parts = out_grad.reshape(NPARTS, ROWS, D)
    gain = ln_gain.astype(jnp.float32)

    def key_terms(pieces):
        features, alive_rows = pieces
        queries, key_rows, value_rows = project(features, w_qkv)
        key_map = heads_of(feature_map(key_rows)) * alive_rows[:, None, None]
        kv_term = jnp.einsum('rhi,rhj->hij', key_map, heads_of(value_rows), precision=highest)
        return (kv_term, lax.optimization_barrier(jnp.sum(key_map, axis=0)))
    kv_terms, ks_terms = lax.map(key_terms, (feats, alive))
    kv_sum = lax.optimization_barrier(jnp.sum(kv_terms, axis=0))
    ks_sum = lax.optimization_barrier(jnp.sum(ks_terms, axis=0))

    def local_pass(pieces):
        features, alive_rows, left, right, nbr_rows, count_rows, grad_rows = pieces
        queries, key_rows, value_rows = project(features, w_qkv)
        query_map = heads_of(feature_map(queries))
        key_map = heads_of(feature_map(key_rows)) * alive_rows[:, None, None]
        value_heads = heads_of(value_rows)
        numer = value_heads + factor * jnp.einsum('rhi,hij->rhj', query_map, kv_sum, precision=highest)
        denom = 1.0 + factor * lax.optimization_barrier(jnp.sum(query_map * ks_sum[None], axis=-1))
        attn = numer / denom[:, :, None]
        agg = combine_rows(features, left, right, nbr_rows, count_rows)
        graph = jnp.dot(agg, w_graph, preferred_element_type=jnp.float32)
        mixed = 0.5 * attn.reshape(ROWS, D) + 0.5 * graph
        mean = lax.optimization_barrier(jnp.sum(mixed, -1, keepdims=True)) / D
        spread = lax.optimization_barrier(jnp.sum(mixed * mixed, -1, keepdims=True)) / D - mean * mean
        rstd = lax.rsqrt(spread + 1e-05)
        normed = (mixed - mean) * rstd
        node_out = (normed * gain[None] * alive_rows[:, None]).astype(jnp.bfloat16)
        dnormed = grad_rows.astype(jnp.float32) * alive_rows[:, None] * gain[None]
        dmixed = rstd * (dnormed - lax.optimization_barrier(jnp.sum(dnormed, -1, keepdims=True)) / D - normed * lax.optimization_barrier(jnp.sum(dnormed * normed, -1, keepdims=True)) / D)
        dgraph = (0.5 * dmixed).astype(jnp.bfloat16)
        graph_term = jnp.einsum('rd,rc->dc', agg, dgraph, preferred_element_type=jnp.float32)
        dattn = heads_of(0.5 * dmixed)
        dnum = dattn / denom[:, :, None]
        dden = -lax.optimization_barrier(jnp.sum(dattn * attn, -1)) / denom
        dkv = factor * jnp.einsum('rhi,rhj->hij', query_map, dnum, precision=highest)
        dks = factor * lax.optimization_barrier(jnp.sum(query_map * dden[:, :, None], axis=0))
        return (node_out, graph_term, dkv, dks, (queries, key_rows, key_map, value_heads, dnum, dden))
    all_pieces = (feats, alive, from_left, from_right, nbr_parts, count_parts, grad_parts)
    outs, graph_terms, dkv_terms, dks_terms = lax.map(lambda pieces: local_pass(pieces)[:4], all_pieces)
    dkv_sum = lax.optimization_barrier(jnp.sum(dkv_terms, axis=0))
    dks_sum = lax.optimization_barrier(jnp.sum(dks_terms, axis=0))

    def weight_terms(pieces):
        features, alive_rows = (pieces[0], pieces[1])
        queries, key_rows, key_map, value_heads, dnum, dden = local_pass(pieces)[4]
        dquery = factor * (jnp.einsum('rhj,hij->rhi', dnum, kv_sum, precision=highest) + dden[:, :, None] * ks_sum[None])
        dvalue = dnum + jnp.einsum('rhi,hij->rhj', key_map, dkv_sum, precision=highest)
        dkey = (jnp.einsum('rhj,hij->rhi', value_heads, dkv_sum, precision=highest) + dks_sum[None]) * alive_rows[:, None, None]
        dprojs = jnp.stack([dquery.reshape(ROWS, D) * feature_slope(queries), dkey.reshape(ROWS, D) * feature_slope(key_rows), dvalue.reshape(ROWS, D)]).astype(jnp.bfloat16)
        return jnp.einsum('rd,krc->kdc', features, dprojs, preferred_element_type=jnp.float32)
    qkv_terms = lax.map(weight_terms, all_pieces)
    loss_scale = lax.rsqrt(total_live)
    qkv_grad = lax.optimization_barrier(jnp.sum(qkv_terms, axis=0)) * loss_scale
    graph_grad = lax.optimization_barrier(jnp.sum(graph_terms, axis=0)) * loss_scale
    return (outs.reshape(NODES, D), qkv_grad, graph_grad)
```

```python
import functools

import jax
import jax.numpy as jnp
from jax import lax
from jax.experimental import pallas as pl
from jax.experimental.pallas import tpu as pltpu
from jax.sharding import Mesh, PartitionSpec as P

D = 256
DH = 32
HEADS = D // DH
TILE = 8
PACK = 5 * D
BLOCK = 128
MESH_FACTORS = {64: (4, 8, 2), 8: (2, 2, 2)}
FINE = ("x", "y", "c", "z")
HIGHEST = lax.Precision.HIGHEST
ROWS_FIRST = (((0,), (0,)), ((), ()))
COLS_LAST = (((1,), (1,)), ((), ()))


def dot(a, b, dims=(((1,), (0,)), ((), ())), precision=None):
    return lax.dot_general(a, b, dims, precision=precision, preferred_element_type=jnp.float32)


def feature_map(value):
    return jnp.where(value > 0, value + 1.0, jnp.exp(jnp.minimum(value, 0.0)))


def feature_slope(value):
    return jnp.where(value > 0, jnp.ones_like(value), jnp.exp(jnp.minimum(value, 0.0)))


def same_head():
    row = lax.broadcasted_iota(jnp.int32, (D, D), 0) // DH
    col = lax.broadcasted_iota(jnp.int32, (D, D), 1) // DH
    return row == col


def alive_of(count, rows, first):
    return (lax.broadcasted_iota(jnp.int32, (rows, 1), 0) + first < count).astype(jnp.float32)


def pack_sums(dense, vectors):
    kept = jnp.where(same_head(), dense, 0.0)
    folded = kept[0:DH]
    for h in range(1, HEADS):
        folded = folded + kept[h * DH : (h + 1) * DH]
    row = lax.broadcasted_iota(jnp.int32, (TILE, D), 0)
    last = jnp.zeros((TILE, D), jnp.float32)
    for i, vector in enumerate(vectors):
        last = jnp.where(row == i, vector, last)
    return [folded[t * TILE : (t + 1) * TILE] for t in range(4)] + [last]


def unpack_sums(packed):
    folded = jnp.concatenate([packed[:, t * D : (t + 1) * D] for t in range(4)], axis=0)
    dense = jnp.where(same_head(), jnp.concatenate([folded] * HEADS, axis=0), 0.0)
    return dense, packed[:, 4 * D : 5 * D]


def key_kernel(count_ref, feats_ref, all_ref, w_ref, send_ref, packed_ref, before_ref, after_ref, kv_ref, ks_ref):
    step = pl.program_id(0)
    rows = feats_ref.shape[0]

    @pl.when(step == 0)
    def _():
        kv_ref[...] = jnp.zeros_like(kv_ref)
        ks_ref[...] = jnp.zeros_like(ks_ref)
        source = all_ref[...]
        slot = lax.broadcasted_iota(jnp.int32, (source.shape[0], send_ref.shape[2]), 0)
        for side, out in ((0, before_ref), (1, after_ref)):
            chosen = (slot == send_ref[0, side : side + 1, :]).astype(jnp.bfloat16)
            out[...] = dot(chosen, source, ROWS_FIRST).astype(jnp.bfloat16)

    feats = feats_ref[...]
    alive = alive_of(count_ref[0], rows, step * rows)
    key_map = feature_map(dot(feats, w_ref[1])) * alive
    value_rows = dot(feats, w_ref[2])
    kv_ref[...] += dot(key_map, value_rows, ROWS_FIRST, HIGHEST)
    ks_ref[...] += jnp.sum(key_map, axis=0, keepdims=True)

    @pl.when(step == pl.num_programs(0) - 1)
    def _():
        live = jnp.full((1, D), count_ref[0].astype(jnp.float32))
        for t, part in enumerate(pack_sums(kv_ref[...], [ks_ref[0:1], live])):
            packed_ref[:, t * D : (t + 1) * D] = part


def agg_kernel(nbr_ref, count_ref, feats_ref, left_ref, right_ref, agg_ref, hits_ref, count_col_ref):
    total = feats_ref.shape[0]
    rim = left_ref.shape[0]
    wide = total + 2 * rim
    sub = 32
    lane = lax.broadcasted_iota(jnp.int32, (128, 128), 1)
    sublane = lax.broadcasted_iota(jnp.int32, (128, 128), 0)
    for b in range(total // 128):
        row = jnp.broadcast_to(count_ref[b : b + 1, :], (128, 128))
        column = jnp.sum(jnp.where(lane == sublane, row, 0), axis=1, keepdims=True)
        count_col_ref[b * 128 : (b + 1) * 128, :] = column
    slots = nbr_ref.shape[1]

    def body(i, carry):
        first = pl.multiple_of(i * sub, sub)
        counts = count_col_ref[pl.ds(first, sub), :]
        slot = lax.broadcasted_iota(jnp.int32, (sub, slots), 1)
        named = jnp.where(slot < counts, nbr_ref[pl.ds(first, sub), :], -1)
        place = lax.broadcasted_iota(jnp.int32, (sub, wide), 1)
        own = lax.broadcasted_iota(jnp.int32, (sub, wide), 0) + first
        hits = (place == own).astype(jnp.float32)
        for s in range(slots):
            hits = hits + (place == named[:, s : s + 1]).astype(jnp.float32)
        hits_ref[pl.ds(first, sub), :] = hits.astype(jnp.bfloat16)
        return carry

    lax.fori_loop(0, total // sub, body, 0)
    summed = dot(hits_ref[:, :total], feats_ref[...])
    summed += dot(hits_ref[:, total : total + rim], left_ref[...])
    summed += dot(hits_ref[:, total + rim :], right_ref[...])
    agg_ref[...] = (summed / (1.0 + count_col_ref[...].astype(jnp.float32))).astype(jnp.bfloat16)


def mix_kernel(
    count_ref, packed_ref, feats_ref, agg_ref, grad_ref, w_ref, wg_ref, gain_ref,
    out_ref, dnum_ref, packed_out_ref, q_term_ref, g_term_ref, kv_ref, dkv_ref, dks_ref,
):
    step = pl.program_id(0)
    rows = feats_ref.shape[0]

    @pl.when(step == 0)
    def _():
        kv_ref[...] = unpack_sums(packed_ref[...])[0]
        dkv_ref[...] = jnp.zeros_like(dkv_ref)
        dks_ref[...] = jnp.zeros_like(dks_ref)
        q_term_ref[...] = jnp.zeros_like(q_term_ref)
        g_term_ref[...] = jnp.zeros_like(g_term_ref)

    ks = packed_ref[0:1, 4 * D : 5 * D]
    live = packed_ref[1:2, 4 * D : 5 * D]
    factor = 1.0 / (DH * live)
    kv = kv_ref[...]
    heads = same_head().astype(jnp.float32)
    gain = gain_ref[...]
    feats = feats_ref[...]
    agg = agg_ref[...]
    alive = alive_of(count_ref[0], rows, step * rows)

    queries = dot(feats, w_ref[0])
    value_rows = dot(feats, w_ref[2])
    query_map = feature_map(queries)
    numer = value_rows + factor * dot(query_map, kv, precision=HIGHEST)
    denom = 1.0 + factor * dot(query_map * ks, heads, precision=HIGHEST)
    inverse = 1.0 / denom
    attn = numer * inverse
    mixed = 0.5 * attn + 0.5 * dot(agg, wg_ref[...])
    mean = jnp.sum(mixed, -1, keepdims=True) / D
    spread = jnp.sum(mixed * mixed, -1, keepdims=True) / D - mean * mean
    rstd = lax.rsqrt(spread + 1e-05)
    normed = (mixed - mean) * rstd
    out_ref[...] = (normed * gain * alive).astype(jnp.bfloat16)
    dnormed = grad_ref[...].astype(jnp.float32) * alive * gain
    dmixed = rstd * (
        dnormed
        - jnp.sum(dnormed, -1, keepdims=True) / D
        - normed * (jnp.sum(dnormed * normed, -1, keepdims=True) / D)
    )
    dattn = 0.5 * dmixed
    g_term_ref[...] += dot(agg, dattn.astype(jnp.bfloat16), ROWS_FIRST)
    dnum = dattn * inverse
    dnum_ref[...] = dnum
    dden = -dot(dattn * attn, heads, precision=HIGHEST) * inverse
    dkv_ref[...] += dot(query_map, dnum, ROWS_FIRST, HIGHEST)
    dks_ref[...] += jnp.sum(query_map * dden, axis=0, keepdims=True)
    dquery = factor * (dot(dnum, kv, COLS_LAST, HIGHEST) + dden * ks) * feature_slope(queries)
    q_term_ref[...] += dot(feats, dquery.astype(jnp.bfloat16), ROWS_FIRST)

    @pl.when(step == pl.num_programs(0) - 1)
    def _():
        for t, part in enumerate(pack_sums(factor * dkv_ref[...], [factor * dks_ref[0:1]])):
            packed_out_ref[:, t * D : (t + 1) * D] = part


def grad_kernel(count_ref, packed_ref, feats_ref, dnum_ref, w_ref, q_term_ref, g_term_ref, terms_ref, dkv_ref):
    step = pl.program_id(0)
    rows = feats_ref.shape[0]

    @pl.when(step == 0)
    def _():
        dkv_ref[...] = unpack_sums(packed_ref[...])[0]
        terms_ref[0] = q_term_ref[...]
        terms_ref[1] = jnp.zeros((D, D), jnp.float32)
        terms_ref[2] = jnp.zeros((D, D), jnp.float32)
        terms_ref[3] = g_term_ref[...]

    dks = packed_ref[0:1, 4 * D : 5 * D]
    dkv = dkv_ref[...]
    feats = feats_ref[...]
    alive = alive_of(count_ref[0], rows, step * rows)
    key_rows = dot(feats, w_ref[1])
    value_rows = dot(feats, w_ref[2])
    key_map = feature_map(key_rows) * alive
    dvalue = dnum_ref[...] + dot(key_map, dkv, precision=HIGHEST)
    dkey = (dot(value_rows, dkv, COLS_LAST, HIGHEST) + dks) * alive * feature_slope(key_rows)
    terms_ref[1] += dot(feats, dkey.astype(jnp.bfloat16), ROWS_FIRST)
    terms_ref[2] += dot(feats, dvalue.astype(jnp.bfloat16), ROWS_FIRST)


def scatter_sum(value, axes, count):
    parts = lax.all_to_all(value, axes, 0, 0, tiled=True)
    return jnp.sum(parts.reshape(count, value.shape[0] // count, *value.shape[1:]), axis=0)


def gather(value, axes, count):
    copies = jnp.broadcast_to(value[None], (count, *value.shape)).reshape(count * value.shape[0], *value.shape[1:])
    return lax.all_to_all(copies, axes, 0, 0, tiled=True)


def sum_packed(packed, sizes):
    near = sizes["x"] * sizes["c"]
    far = sizes["y"] * sizes["z"]
    share = scatter_sum(packed.reshape(TILE, PACK), ("x", "c"), near)
    share = jnp.sum(gather(share, ("y", "z"), far).reshape(far, *share.shape), axis=0)
    return gather(share, ("x", "c"), near)


def sum_terms(terms, sizes, scale):
    far = sizes["y"] * sizes["z"]
    value = scatter_sum(terms, "c", sizes["c"])
    value = scatter_sum(value, "x", sizes["x"])
    value = scatter_sum(value, ("y", "z"), far) * scale
    value = gather(value, ("y", "z"), far)
    value = gather(value, "x", sizes["x"])
    return gather(value, "c", sizes["c"])


def local(sizes, node_feats, w_qkv, w_graph, ln_gain, out_grad, part_counts, send_rows, neighbours, neighbour_counts):
    rows = node_feats.shape[0]
    rim = send_rows.shape[2]
    steps = rows // BLOCK
    f32, bf16 = jnp.float32, jnp.bfloat16
    smem = pl.BlockSpec(memory_space=pltpu.SMEM)

    def whole(*shape):
        return pl.BlockSpec(shape, lambda i: (0,) * len(shape))

    by_row = pl.BlockSpec((BLOCK, D), lambda i: (i, 0))
    shape = jax.ShapeDtypeStruct

    packed, to_before, to_after = pl.pallas_call(
        key_kernel,
        grid=(steps,),
        in_specs=[smem, by_row, whole(rows, D), whole(3, D, D), whole(1, 2, rim)],
        out_specs=[whole(TILE, PACK), whole(rim, D), whole(rim, D)],
        out_shape=[shape((TILE, PACK), f32), shape((rim, D), bf16), shape((rim, D), bf16)],
        scratch_shapes=[pltpu.VMEM((D, D), f32), pltpu.VMEM((1, D), f32)],
        name="keys",
    )(part_counts, node_feats, node_feats, w_qkv, send_rows)

    parts = sizes["x"] * sizes["y"] * sizes["c"] * sizes["z"]
    up = [(i, i + 1) for i in range(parts - 1)]
    down = [(j, i) for i, j in up]
    left = lax.ppermute(to_after, FINE, up)
    right = lax.ppermute(to_before, FINE, down)
    packed = sum_packed(packed, sizes)

    agg = pl.pallas_call(
        agg_kernel,
        out_shape=shape((rows, D), bf16),
        scratch_shapes=[pltpu.VMEM((rows, rows + 2 * rim), bf16), pltpu.VMEM((rows, 1), jnp.int32)],
        name="aggregate",
    )(neighbours, neighbour_counts.reshape(rows // 128, 128), node_feats, left, right)

    node_out, dnum, dpacked, q_term, g_term = pl.pallas_call(
        mix_kernel,
        grid=(steps,),
        in_specs=[smem, whole(TILE, PACK), by_row, by_row, by_row, whole(3, D, D), whole(D, D), whole(1, D)],
        out_specs=[by_row, by_row, whole(TILE, PACK), whole(D, D), whole(D, D)],
        out_shape=[
            shape((rows, D), bf16), shape((rows, D), f32), shape((TILE, PACK), f32),
            shape((D, D), f32), shape((D, D), f32),
        ],
        scratch_shapes=[pltpu.VMEM((D, D), f32), pltpu.VMEM((D, D), f32), pltpu.VMEM((1, D), f32)],
        name="mix",
    )(part_counts, packed, node_feats, agg, out_grad, w_qkv, w_graph, ln_gain.reshape(1, D))

    dpacked = sum_packed(dpacked, sizes)

    terms = pl.pallas_call(
        grad_kernel,
        grid=(steps,),
        in_specs=[smem, whole(TILE, PACK), by_row, by_row, whole(3, D, D), whole(D, D), whole(D, D)],
        out_specs=whole(4, D, D),
        out_shape=shape((4, D, D), f32),
        scratch_shapes=[pltpu.VMEM((D, D), f32)],
        name="grads",
    )(part_counts, dpacked, node_feats, dnum, w_qkv, q_term, g_term)

    scale = lax.rsqrt(packed[1:2, 4 * D : 4 * D + 1])
    total = sum_terms(terms.reshape(4 * D, D), sizes, scale).reshape(4, D, D)
    return node_out, total[:3], total[3]


def solution(mesh):
    sizes = dict(zip(FINE, (*MESH_FACTORS[mesh.shape["dom"]], mesh.shape["head"])))
    fine = Mesh(mesh.devices.reshape(tuple(sizes.values())), FINE)
    return jax.shard_map(
        functools.partial(local, sizes),
        mesh=fine,
        in_specs=(
            P(FINE, None), P(), P(), P(), P(FINE, None), P(FINE), P(FINE, None, None), P(FINE, None), P(FINE),
        ),
        out_specs=(P(FINE, None), P(), P()),
        check_vma=False,
    )
```

```python
import functools

import jax
import jax.numpy as jnp
from jax import lax
from jax.experimental import pallas as pl
from jax.experimental.pallas import tpu as pltpu
from jax.sharding import Mesh, PartitionSpec as P

D = 256
DH = 32
HEADS = D // DH
TILE = 8
PACK = 5 * D
BLOCK = 128
MESH_FACTORS = {64: (4, 8, 2), 8: (2, 2, 2)}
FINE = ("x", "y", "c", "z")
ROWS_FIRST = (((0,), (0,)), ((), ()))
COLS_LAST = (((1,), (1,)), ((), ()))


def dot(a, b, dims=(((1,), (0,)), ((), ()))):
    return lax.dot_general(a, b, dims, preferred_element_type=jnp.float32)


def feature_map(value):
    return jnp.where(value > 0, value + 1.0, jnp.exp(jnp.minimum(value, 0.0)))


def same_head():
    row = lax.broadcasted_iota(jnp.int32, (D, D), 0) // DH
    col = lax.broadcasted_iota(jnp.int32, (D, D), 1) // DH
    return row == col


def alive_of(count, rows, first):
    return (lax.broadcasted_iota(jnp.int32, (rows, 1), 0) + first < count).astype(jnp.float32)


def store_packed(out_ref, dense, vectors):
    kept = jnp.where(same_head(), dense, 0.0)
    folded = kept[0:DH]
    for h in range(1, HEADS):
        folded = folded + kept[h * DH : (h + 1) * DH]
    row = lax.broadcasted_iota(jnp.int32, (TILE, D), 0)
    last = jnp.zeros((TILE, D), jnp.float32)
    for i, vector in enumerate(vectors):
        last = jnp.where(row == i, vector, last)
    tiles = [folded[t * TILE : (t + 1) * TILE] for t in range(4)] + [last]
    for t, tile in enumerate(tiles):
        for r in range(TILE):
            out_ref[r, :, t * D : (t + 1) * D] = tile[r : r + 1]


def load_packed(packed_ref):
    tiles = [
        jnp.concatenate([packed_ref[r, :, t * D : (t + 1) * D] for r in range(TILE)], axis=0) for t in range(5)
    ]
    folded = jnp.concatenate(tiles[:4], axis=0)
    return jnp.where(same_head(), jnp.concatenate([folded] * HEADS, axis=0), 0.0), tiles[4]


def halves(value):
    high = value.astype(jnp.bfloat16)
    return high, (value - high.astype(jnp.float32)).astype(jnp.bfloat16)


def dot3(a, b, dims=(((1,), (0,)), ((), ()))):
    return dot(a[0], b[0], dims) + (dot(a[0], b[1], dims) + dot(a[1], b[0], dims))


def head_sums(value, heads):
    high, low = halves(value)
    return dot(high, heads) + dot(low, heads)


def key_kernel(
    count_ref, feats_ref, all_ref, w_ref, send_ref,
    packed_ref, before_ref, after_ref, key_ref, value_ref, kv_ref, ks_ref,
):
    step = pl.program_id(0)
    rows = feats_ref.shape[0]

    @pl.when(step == 0)
    def _():
        kv_ref[...] = jnp.zeros_like(kv_ref)
        ks_ref[...] = jnp.zeros_like(ks_ref)
        source = all_ref[...]
        slot = lax.broadcasted_iota(jnp.int32, (source.shape[0], send_ref.shape[2]), 0)
        for side, out in ((0, before_ref), (1, after_ref)):
            chosen = (slot == send_ref[0, side : side + 1, :]).astype(jnp.bfloat16)
            out[...] = dot(chosen, source, ROWS_FIRST).astype(jnp.bfloat16)

    feats = feats_ref[...]
    alive = alive_of(count_ref[0], rows, step * rows)
    key_map = feature_map(dot(feats, w_ref[1]))
    value_rows = dot(feats, w_ref[2])
    key_ref[...] = key_map
    value_ref[...] = value_rows
    key_map = key_map * alive
    kv_ref[...] += dot3(halves(key_map), halves(value_rows), ROWS_FIRST)
    ks_ref[...] += jnp.sum(key_map, axis=0, keepdims=True)

    @pl.when(step == pl.num_programs(0) - 1)
    def _():
        live = jnp.full((1, D), count_ref[0].astype(jnp.float32))
        store_packed(packed_ref, kv_ref[...], [ks_ref[...], live])


def prep_kernel(nbr_ref, count_ref, feats_ref, left_ref, right_ref, w_ref, wg_ref, agg_ref, graph_ref, query_ref, hits_ref):
    total = feats_ref.shape[0]
    rim = left_ref.shape[0]
    wide = total + 2 * rim
    slots = nbr_ref.shape[0]
    sub = 32
    for b in range(total // 128):
        at = slice(b * 128, (b + 1) * 128)
        slot = lax.broadcasted_iota(jnp.int32, (slots, 128), 0)
        named = jnp.where(slot < count_ref[:, at], nbr_ref[:, at], -1)
        rows = [jnp.broadcast_to(named[s : s + 1], (sub, 128)) for s in range(slots)]
        own = lax.broadcasted_iota(jnp.int32, (sub, 128), 1) + b * 128
        place0 = lax.broadcasted_iota(jnp.int32, (sub, 128), 0)

        def body(i, carry):
            first = pl.multiple_of(i * sub, sub)
            place = place0 + first
            hits = (place == own).astype(jnp.float32)
            for s in range(slots):
                hits = hits + (place == rows[s]).astype(jnp.float32)
            hits_ref[pl.ds(first, sub), at] = hits.astype(jnp.bfloat16)
            return carry

        lax.fori_loop(0, wide // sub, body, 0)
    ones = jnp.ones((wide, 128), jnp.bfloat16)
    for b in range(total // 128):
        at = slice(b * 128, (b + 1) * 128)
        summed = dot(hits_ref[:total, at], feats_ref[...], ROWS_FIRST)
        summed += dot(hits_ref[total : total + rim, at], left_ref[...], ROWS_FIRST)
        summed += dot(hits_ref[total + rim :, at], right_ref[...], ROWS_FIRST)
        named = dot(hits_ref[:, at], ones, ROWS_FIRST)
        agg = (summed / jnp.concatenate([named, named], axis=1)).astype(jnp.bfloat16)
        agg_ref[at, :] = agg
        graph_ref[at, :] = dot(agg, wg_ref[...])
        query_ref[at, :] = feature_map(dot(feats_ref[at, :], w_ref[0]))


def mix_kernel(
    count_ref, packed_ref, query_ref, value_ref, graph_ref, grad_ref, gain_ref,
    out_ref, dgraph_ref, dnum_ref, dden_ref, packed_out_ref, kv_ref, vec_ref, dkv_ref, dks_ref,
):
    step = pl.program_id(0)
    rows = query_ref.shape[0]

    @pl.when(step == 0)
    def _():
        kv, vectors = load_packed(packed_ref)
        kv_ref[0], kv_ref[1] = halves(kv)
        vec_ref[...] = vectors
        dkv_ref[...] = jnp.zeros_like(dkv_ref)
        dks_ref[...] = jnp.zeros_like(dks_ref)

    ks = vec_ref[0:1]
    factor = 1.0 / (DH * vec_ref[1:2])
    heads = same_head().astype(jnp.bfloat16)
    gain = gain_ref[...]
    alive = alive_of(count_ref[0], rows, step * rows)

    query_map = query_ref[...]
    query_halves = halves(query_map)
    numer = value_ref[...] + factor * dot3(query_halves, (kv_ref[0], kv_ref[1]))
    denom = 1.0 + factor * head_sums(query_map * ks, heads)
    inverse = 1.0 / denom
    attn = numer * inverse
    mixed = 0.5 * attn + 0.5 * graph_ref[...]
    mean = jnp.sum(mixed, -1, keepdims=True) / D
    spread = jnp.sum(mixed * mixed, -1, keepdims=True) / D - mean * mean
    rstd = lax.rsqrt(spread + 1e-05)
    normed = (mixed - mean) * rstd
    gain_alive = gain * alive
    out_ref[...] = (normed * gain_alive).astype(jnp.bfloat16)
    dnormed = grad_ref[...].astype(jnp.float32) * gain_alive
    dmixed = rstd * (
        dnormed
        - jnp.sum(dnormed, -1, keepdims=True) / D
        - normed * (jnp.sum(dnormed * normed, -1, keepdims=True) / D)
    )
    dattn = 0.5 * dmixed
    dgraph_ref[...] = dattn.astype(jnp.bfloat16)
    dnum = dattn * inverse
    dnum_ref[...] = dnum
    dden = -head_sums(dattn * attn, heads) * inverse
    dden_ref[...] = dden
    dkv_ref[...] += dot3(query_halves, halves(dnum), ROWS_FIRST)
    dks_ref[...] += jnp.sum(query_map * dden, axis=0, keepdims=True)

    @pl.when(step == pl.num_programs(0) - 1)
    def _():
        store_packed(packed_out_ref, factor * dkv_ref[...], [factor * dks_ref[...]])


def query_kernel(packed_ref, feats_ref, agg_ref, query_ref, dgraph_ref, dnum_ref, dden_ref, terms_ref, kv_ref, vec_ref):
    step = pl.program_id(0)

    @pl.when(step == 0)
    def _():
        kv, vectors = load_packed(packed_ref)
        kv_ref[0], kv_ref[1] = halves(kv)
        vec_ref[...] = vectors
        terms_ref[...] = jnp.zeros_like(terms_ref)

    factor = 1.0 / (DH * vec_ref[1:2])
    slope = jnp.minimum(query_ref[...], 1.0)
    dquery = factor * (
        dot3(halves(dnum_ref[...]), (kv_ref[0], kv_ref[1]), COLS_LAST) + dden_ref[...] * vec_ref[0:1]
    ) * slope
    terms_ref[0] += dot(agg_ref[...], dgraph_ref[...], ROWS_FIRST)
    terms_ref[1] += dot(feats_ref[...], dquery.astype(jnp.bfloat16), ROWS_FIRST)


def grad_kernel(count_ref, packed_ref, feats_ref, key_ref, value_ref, dnum_ref, held_ref, terms_ref, kv_ref, vec_ref):
    del held_ref
    step = pl.program_id(0)
    rows = feats_ref.shape[0]

    @pl.when(step == 0)
    def _():
        dkv, vectors = load_packed(packed_ref)
        kv_ref[0], kv_ref[1] = halves(dkv)
        vec_ref[...] = vectors
        terms_ref[...] = jnp.zeros_like(terms_ref)

    dkv = (kv_ref[0], kv_ref[1])
    feats = feats_ref[...]
    alive = alive_of(count_ref[0], rows, step * rows)
    key_map = key_ref[...]
    slope = jnp.minimum(key_map, 1.0) * alive
    dvalue = dnum_ref[...] + dot3(halves(key_map * alive), dkv)
    dkey = (dot3(halves(value_ref[...]), dkv, COLS_LAST) + vec_ref[0:1]) * slope
    terms_ref[0] += dot(feats, dkey.astype(jnp.bfloat16), ROWS_FIRST)
    terms_ref[1] += dot(feats, dvalue.astype(jnp.bfloat16), ROWS_FIRST)


def scatter_sum(value, axes, count):
    parts = lax.all_to_all(value, axes, 0, 0, tiled=True)
    return jnp.sum(parts.reshape(count, value.shape[0] // count, *value.shape[1:]), axis=0)


def gather(value, axes, count):
    copies = jnp.broadcast_to(value[None], (count, *value.shape)).reshape(count * value.shape[0], *value.shape[1:])
    return lax.all_to_all(copies, axes, 0, 0, tiled=True)


def gather_sum(value, axes, count):
    return jnp.sum(gather(value, axes, count).reshape(count, *value.shape), axis=0)


def sum_terms(terms, sizes, scale):
    value = scatter_sum(terms, "c", sizes["c"])
    value = scatter_sum(value, "x", sizes["x"])
    value = scatter_sum(value, "y", sizes["y"])
    value = gather_sum(value, "z", sizes["z"]) * scale
    value = gather(value, "y", sizes["y"])
    value = gather(value, "x", sizes["x"])
    return gather(value, "c", sizes["c"])


def local(sizes, node_feats, w_qkv, w_graph, ln_gain, out_grad, part_counts, send_rows, neighbours, neighbour_counts):
    rows = node_feats.shape[0]
    rim = send_rows.shape[2]
    steps = rows // BLOCK
    near = sizes["x"] * sizes["c"]
    parts = near * sizes["y"] * sizes["z"]
    f32, bf16 = jnp.float32, jnp.bfloat16
    smem = pl.BlockSpec(memory_space=pltpu.SMEM)
    shape = jax.ShapeDtypeStruct

    def whole(*shape):
        return pl.BlockSpec(shape, lambda i: (0,) * len(shape))

    by_row = pl.BlockSpec((BLOCK, D), lambda i: (i, 0))
    rows_f32, rows_bf16 = shape((rows, D), f32), shape((rows, D), bf16)
    packed_whole, packed_shape = whole(TILE, 1, PACK), shape((TILE, 1, PACK), f32)
    kv_halves, vectors = pltpu.VMEM((2, D, D), bf16), pltpu.VMEM((TILE, D), f32)

    packed, to_before, to_after, key_map, value_rows = pl.pallas_call(
        key_kernel,
        grid=(steps,),
        in_specs=[smem, by_row, whole(rows, D), whole(3, D, D), whole(1, 2, rim)],
        out_specs=[packed_whole, whole(rim, D), whole(rim, D), by_row, by_row],
        out_shape=[packed_shape, shape((rim, D), bf16), shape((rim, D), bf16), rows_f32, rows_f32],
        scratch_shapes=[pltpu.VMEM((D, D), f32), pltpu.VMEM((1, D), f32)],
        name="keys",
    )(part_counts, node_feats, node_feats, w_qkv, send_rows)

    up = [(i, i + 1) for i in range(parts - 1)]
    down = [(j, i) for i, j in up]
    share = scatter_sum(packed, ("x", "c"), near)
    left = lax.ppermute(to_after, FINE, up)
    right = lax.ppermute(to_before, FINE, down)
    share = gather_sum(share, "y", sizes["y"])
    share, left, right = lax.optimization_barrier((share, left, right))
    agg, graph, query_map = pl.pallas_call(
        prep_kernel,
        out_shape=[rows_bf16, rows_f32, rows_f32],
        scratch_shapes=[pltpu.VMEM((rows + 2 * rim, rows), bf16)],
        cost_estimate=pl.CostEstimate(flops=10**9, bytes_accessed=10**7, transcendentals=0),
        name="prepare",
    )(neighbours.T, neighbour_counts.reshape(1, rows), node_feats, left, right, w_qkv, w_graph)
    share = gather_sum(share, "z", sizes["z"])
    share, agg, graph, query_map = lax.optimization_barrier((share, agg, graph, query_map))
    packed = gather(share, ("x", "c"), near)

    node_out, dgraph, dnum, dden, dpacked = pl.pallas_call(
        mix_kernel,
        grid=(steps,),
        in_specs=[smem, packed_whole, by_row, by_row, by_row, by_row, whole(1, D)],
        out_specs=[by_row, by_row, by_row, by_row, packed_whole],
        out_shape=[rows_bf16, rows_bf16, rows_f32, rows_f32, packed_shape],
        scratch_shapes=[kv_halves, vectors, pltpu.VMEM((D, D), f32), pltpu.VMEM((1, D), f32)],
        name="mix",
    )(part_counts, packed, query_map, value_rows, graph, out_grad, ln_gain.reshape(1, D))

    share = scatter_sum(dpacked, ("x", "c"), near)
    share = gather_sum(share, "y", sizes["y"])
    terms = pl.pallas_call(
        query_kernel,
        grid=(steps,),
        in_specs=[packed_whole, by_row, by_row, by_row, by_row, by_row, by_row],
        out_specs=whole(2, D, D),
        out_shape=shape((4, D, D), f32),
        scratch_shapes=[kv_halves, vectors],
        cost_estimate=pl.CostEstimate(flops=10**9, bytes_accessed=10**7, transcendentals=0),
        name="queries",
    )(packed, node_feats, agg, query_map, dgraph, dnum, dden)
    share = gather_sum(share, "z", sizes["z"])
    share, terms = lax.optimization_barrier((share, terms))
    dpacked = gather(share, ("x", "c"), near)

    terms = pl.pallas_call(
        grad_kernel,
        grid=(steps,),
        in_specs=[smem, packed_whole, by_row, by_row, by_row, by_row, pl.BlockSpec(memory_space=pl.ANY)],
        out_specs=pl.BlockSpec((2, D, D), lambda i: (1, 0, 0)),
        out_shape=shape((4, D, D), f32),
        scratch_shapes=[kv_halves, vectors],
        input_output_aliases={6: 0},
        name="grads",
    )(part_counts, dpacked, node_feats, key_map, value_rows, dnum, terms)

    scale = lax.rsqrt(packed[1, :, 4 * D : 4 * D + 1])
    total = sum_terms(terms.reshape(4 * D, D), sizes, scale).reshape(4, D, D)
    return node_out, total[1:], total[0]


def solution(mesh):
    sizes = dict(zip(FINE, (*MESH_FACTORS[mesh.shape["dom"]], mesh.shape["head"])))
    fine = Mesh(mesh.devices.reshape(tuple(sizes.values())), FINE)
    return jax.shard_map(
        functools.partial(local, sizes),
        mesh=fine,
        in_specs=(
            P(FINE, None), P(), P(), P(), P(FINE, None), P(FINE), P(FINE, None, None), P(FINE, None), P(FINE),
        ),
        out_specs=(P(FINE, None), P(), P()),
        check_vma=False,
    )
```

```python
import functools

import jax
import jax.numpy as jnp
from jax import lax
from jax.experimental import pallas as pl
from jax.experimental.pallas import tpu as pltpu
from jax.sharding import Mesh, PartitionSpec as P

D = 256
DH = 32
HEADS = D // DH
TILE = 8
PACK = 5 * D
VMEM_LIMIT = 16 << 20
MESH_FACTORS = {64: (4, 8, 2), 8: (2, 2, 2)}
FINE = ("x", "y", "c", "z")
ROWS_FIRST = (((0,), (0,)), ((), ()))
COLS_LAST = (((1,), (1,)), ((), ()))


def dot(a, b, dims=(((1,), (0,)), ((), ()))):
    return lax.dot_general(a, b, dims, preferred_element_type=jnp.float32)


def feature_map(value):
    return jnp.where(value > 0, value + 1.0, jnp.exp(jnp.minimum(value, 0.0)))


def same_head():
    row = lax.broadcasted_iota(jnp.int32, (D, D), 0) // DH
    col = lax.broadcasted_iota(jnp.int32, (D, D), 1) // DH
    return row == col


def alive_of(count_ref, rows):
    return (lax.broadcasted_iota(jnp.int32, (rows, 1), 0) < count_ref[...]).astype(jnp.float32)


def store_packed(out_ref, dense, vectors):
    kept = jnp.where(same_head(), dense, 0.0)
    folded = kept[0:DH]
    for h in range(1, HEADS):
        folded = folded + kept[h * DH : (h + 1) * DH]
    row = lax.broadcasted_iota(jnp.int32, (TILE, D), 0)
    last = jnp.zeros((TILE, D), jnp.float32)
    for i, vector in enumerate(vectors):
        last = jnp.where(row == i, vector, last)
    tiles = [folded[t * TILE : (t + 1) * TILE] for t in range(4)] + [last]
    for t, tile in enumerate(tiles):
        for r in range(TILE):
            out_ref[r, :, t * D : (t + 1) * D] = tile[r : r + 1]


def load_packed(packed_ref):
    tiles = [
        jnp.concatenate([packed_ref[r, :, t * D : (t + 1) * D] for r in range(TILE)], axis=0) for t in range(5)
    ]
    folded = jnp.concatenate(tiles[:4], axis=0)
    return jnp.where(same_head(), jnp.concatenate([folded] * HEADS, axis=0), 0.0), tiles[4]


def halves(value):
    high = value.astype(jnp.bfloat16)
    return high, (value - high.astype(jnp.float32)).astype(jnp.bfloat16)


def dot3(a, b, dims=(((1,), (0,)), ((), ()))):
    return dot(a[0], b[0], dims) + (dot(a[0], b[1], dims) + dot(a[1], b[0], dims))


def head_sums(value, heads):
    high, low = halves(value)
    return dot(high, heads) + dot(low, heads)


def key_kernel(count_ref, feats_ref, w_ref, send_ref, packed_ref, before_ref, after_ref, key_ref, value_ref):
    feats = feats_ref[...]
    slot = lax.broadcasted_iota(jnp.int32, (feats.shape[0], send_ref.shape[2]), 0)
    for side, out in ((0, before_ref), (1, after_ref)):
        chosen = (slot == send_ref[0, side : side + 1, :]).astype(jnp.bfloat16)
        out[...] = dot(chosen, feats, ROWS_FIRST).astype(jnp.bfloat16)
    key_map = feature_map(dot(feats, w_ref[1]))
    value_rows = dot(feats, w_ref[2])
    key_ref[...] = key_map
    value_ref[...] = value_rows
    key_map = key_map * alive_of(count_ref, feats.shape[0])
    kv = dot3(halves(key_map), halves(value_rows), ROWS_FIRST)
    live = jnp.broadcast_to(count_ref[...].astype(jnp.float32), (1, D))
    store_packed(packed_ref, kv, [jnp.sum(key_map, axis=0, keepdims=True), live])


def hit_kernel(nbr_ref, count_ref, hits_ref):
    wide, total = hits_ref.shape
    slots = nbr_ref.shape[0]
    sub = 32
    for b in range(total // 128):
        at = slice(b * 128, (b + 1) * 128)
        slot = lax.broadcasted_iota(jnp.int32, (slots, 128), 0)
        named = jnp.where(slot < count_ref[:, at], nbr_ref[:, at], -1)
        rows = [jnp.broadcast_to(named[s : s + 1], (sub, 128)) for s in range(slots)]
        own = lax.broadcasted_iota(jnp.int32, (sub, 128), 1) + b * 128
        place0 = lax.broadcasted_iota(jnp.int32, (sub, 128), 0)

        def body(i, carry):
            first = pl.multiple_of(i * sub, sub)
            place = place0 + first
            hits = (place == own).astype(jnp.float32)
            for s in range(slots):
                hits = hits + (place == rows[s]).astype(jnp.float32)
            hits_ref[pl.ds(first, sub), at] = hits.astype(jnp.bfloat16)
            return carry

        lax.fori_loop(0, wide // sub, body, 0)


def graph_kernel(hits_ref, feats_ref, left_ref, right_ref, wg_ref, agg_ref, graph_ref):
    total = feats_ref.shape[0]
    rim = left_ref.shape[0]
    summed = dot(hits_ref[:total, :], feats_ref[...], ROWS_FIRST)
    summed += dot(hits_ref[total : total + rim, :], left_ref[...], ROWS_FIRST)
    summed += dot(hits_ref[total + rim :, :], right_ref[...], ROWS_FIRST)
    named = dot(hits_ref[...], jnp.ones((total + 2 * rim, 128), jnp.bfloat16), ROWS_FIRST)
    agg = (summed / jnp.concatenate([named, named], axis=1)).astype(jnp.bfloat16)
    agg_ref[...] = agg
    graph_ref[...] = 0.5 * dot(agg, wg_ref[...])


def project_kernel(feats_ref, w_ref, query_ref):
    query_ref[...] = feature_map(dot(feats_ref[...], w_ref[0]))


def mix_kernel(
    count_ref, packed_ref, query_ref, value_ref, graph_ref, grad_ref, gain_ref,
    out_ref, dgraph_ref, dnum_ref, dden_ref, packed_out_ref, scale_ref,
):
    kv, vectors = load_packed(packed_ref)
    kv = halves(kv)
    ks, live = vectors[0:1], vectors[1:2]
    factor = 1.0 / (DH * live)
    scale_ref[...] = lax.rsqrt(live)
    heads = same_head().astype(jnp.bfloat16)
    gain_alive = gain_ref[...] * alive_of(count_ref, query_ref.shape[0])

    query_map = query_ref[...]
    query_halves = halves(query_map)
    numer = value_ref[...] + factor * dot3(query_halves, kv)
    denom = 1.0 + factor * head_sums(query_map * ks, heads)
    inverse = 1.0 / denom
    attn = numer * inverse
    mixed = 0.5 * attn + graph_ref[...]
    mean = jnp.sum(mixed, -1, keepdims=True) / D
    spread = jnp.sum(mixed * mixed, -1, keepdims=True) / D - mean * mean
    rstd = lax.rsqrt(spread + 1e-05)
    normed = (mixed - mean) * rstd
    out_ref[...] = (normed * gain_alive).astype(jnp.bfloat16)
    dnormed = grad_ref[...].astype(jnp.float32) * gain_alive
    dmixed = rstd * (
        dnormed
        - jnp.sum(dnormed, -1, keepdims=True) / D
        - normed * (jnp.sum(dnormed * normed, -1, keepdims=True) / D)
    )
    dattn = 0.5 * dmixed
    dgraph_ref[...] = dattn.astype(jnp.bfloat16)
    dnum = dattn * inverse
    dnum_ref[...] = dnum
    dden = -head_sums(dattn * attn, heads) * inverse
    dden_ref[...] = dden
    dkv = dot3(query_halves, halves(dnum), ROWS_FIRST)
    dks = jnp.sum(query_map * dden, axis=0, keepdims=True)
    store_packed(packed_out_ref, factor * dkv, [factor * dks])


def query_kernel(packed_ref, feats_ref, agg_ref, query_ref, dgraph_ref, dnum_ref, dden_ref, terms_ref):
    kv, vectors = load_packed(packed_ref)
    factor = 1.0 / (DH * vectors[1:2])
    slope = jnp.minimum(query_ref[...], 1.0)
    dquery = factor * (dot3(halves(dnum_ref[...]), halves(kv), COLS_LAST) + dden_ref[...] * vectors[0:1]) * slope
    terms_ref[0] = dot(agg_ref[...], dgraph_ref[...], ROWS_FIRST)
    terms_ref[1] = dot(feats_ref[...], dquery.astype(jnp.bfloat16), ROWS_FIRST)


def grad_kernel(count_ref, packed_ref, feats_ref, key_ref, value_ref, dnum_ref, held_ref, terms_ref):
    terms_ref[0] = held_ref[0]
    terms_ref[1] = held_ref[1]
    dkv, vectors = load_packed(packed_ref)
    dkv = halves(dkv)
    feats = feats_ref[...]
    alive = alive_of(count_ref, feats.shape[0])
    key_map = key_ref[...]
    slope = jnp.minimum(key_map, 1.0) * alive
    dvalue = dnum_ref[...] + dot3(halves(key_map * alive), dkv)
    dkey = (dot3(halves(value_ref[...]), dkv, COLS_LAST) + vectors[0:1]) * slope
    terms_ref[2] = dot(feats, dkey.astype(jnp.bfloat16), ROWS_FIRST)
    terms_ref[3] = dot(feats, dvalue.astype(jnp.bfloat16), ROWS_FIRST)


def call(kernel, name, shapes, *args):
    def here(one):
        return pl.BlockSpec(memory_space=pltpu.VMEM)

    return pl.pallas_call(
        kernel,
        in_specs=[here(arg) for arg in args],
        out_specs=jax.tree.map(here, shapes),
        out_shape=shapes,
        cost_estimate=pl.CostEstimate(flops=10**9, bytes_accessed=10**7, transcendentals=0),
        compiler_params=pltpu.CompilerParams(vmem_limit_bytes=VMEM_LIMIT),
        name=name,
    )(*args)


def scatter_sum(value, axes, count):
    parts = lax.all_to_all(value, axes, 0, 0, tiled=True)
    return jnp.sum(parts.reshape(count, value.shape[0] // count, *value.shape[1:]), axis=0)


def gather(value, axes, count):
    copies = jnp.broadcast_to(value[None], (count, *value.shape)).reshape(count * value.shape[0], *value.shape[1:])
    return lax.all_to_all(copies, axes, 0, 0, tiled=True)


def gather_sum(value, axes, count):
    return jnp.sum(gather(value, axes, count).reshape(count, *value.shape), axis=0)


def sum_terms(terms, sizes, scale):
    value = scatter_sum(terms, "c", sizes["c"])
    value = scatter_sum(value, "x", sizes["x"])
    value = scatter_sum(value, "y", sizes["y"])
    value = gather_sum(value, "z", sizes["z"]) * scale
    value = gather(value, "y", sizes["y"])
    value = gather(value, "x", sizes["x"])
    return gather(value, "c", sizes["c"])


def local(sizes, node_feats, w_qkv, w_graph, ln_gain, out_grad, part_counts, send_rows, neighbours, neighbour_counts):
    rows = node_feats.shape[0]
    rim = send_rows.shape[2]
    near = sizes["x"] * sizes["c"]
    parts = near * sizes["y"] * sizes["z"]
    f32, bf16 = jnp.float32, jnp.bfloat16
    shape = jax.ShapeDtypeStruct
    count = part_counts.reshape(1, 1)
    rows_f32, rows_bf16 = shape((rows, D), f32), shape((rows, D), bf16)
    packed_shape, rim_shape = shape((TILE, 1, PACK), f32), shape((rim, D), bf16)
    together = lax.optimization_barrier

    packed, to_before, to_after, key_map, value_rows = call(
        key_kernel, "keys", [packed_shape, rim_shape, rim_shape, rows_f32, rows_f32],
        count, node_feats, w_qkv, send_rows,
    )

    up = [(i, i + 1) for i in range(parts - 1)]
    down = [(j, i) for i, j in up]
    hits = call(
        hit_kernel, "hits", shape((rows + 2 * rim, rows), bf16), neighbours.T, neighbour_counts.reshape(1, rows)
    )
    share = scatter_sum(packed, ("x", "c"), near)
    share, hits, to_before, to_after = together((share, hits, to_before, to_after))
    left = lax.ppermute(to_after, FINE, up)
    right = lax.ppermute(to_before, FINE, down)
    share = gather_sum(share, "y", sizes["y"])
    share, left, right = together((share, left, right))
    agg, graph = call(graph_kernel, "graph", [rows_bf16, rows_f32], hits, node_feats, left, right, w_graph)
    share = gather_sum(share, "z", sizes["z"])
    share, agg, graph, feats_here = together((share, agg, graph, node_feats))
    query_map = call(project_kernel, "project", rows_f32, feats_here, w_qkv)
    packed = gather(share, ("x", "c"), near)

    node_out, dgraph, dnum, dden, dpacked, scale = call(
        mix_kernel, "mix", [rows_bf16, rows_bf16, rows_f32, rows_f32, packed_shape, shape((1, D), f32)],
        count, packed, query_map, value_rows, graph, out_grad, ln_gain.reshape(1, D),
    )

    share = scatter_sum(dpacked, ("x", "c"), near)
    share = gather_sum(share, "y", sizes["y"])
    terms = call(
        query_kernel, "queries", shape((2, D, D), f32), packed, node_feats, agg, query_map, dgraph, dnum, dden
    )
    share = gather_sum(share, "z", sizes["z"])
    share, terms = together((share, terms))
    dpacked = gather(share, ("x", "c"), near)

    terms = call(
        grad_kernel, "grads", shape((4, D, D), f32), count, dpacked, node_feats, key_map, value_rows, dnum, terms
    )

    total = sum_terms(terms.reshape(4 * D, D), sizes, scale).reshape(4, D, D)
    return node_out, total[1:], total[0]


def solution(mesh):
    sizes = dict(zip(FINE, (*MESH_FACTORS[mesh.shape["dom"]], mesh.shape["head"])))
    fine = Mesh(mesh.devices.reshape(tuple(sizes.values())), FINE)
    return jax.shard_map(
        functools.partial(local, sizes),
        mesh=fine,
        in_specs=(
            P(FINE, None), P(), P(), P(), P(FINE, None), P(FINE), P(FINE, None, None), P(FINE, None), P(FINE),
        ),
        out_specs=(P(FINE, None), P(), P()),
        check_vma=False,
    )
```

```python
import functools

import jax
import jax.numpy as jnp
from jax import lax
from jax.experimental import pallas as pl
from jax.experimental.pallas import tpu as pltpu
from jax.sharding import Mesh, PartitionSpec as P

D = 256
DH = 32
HEADS = D // DH
TILE = 8
PACK = 5 * D
VMEM_LIMIT = 16 << 20
MESH_FACTORS = {64: (4, 8, 2), 8: (2, 2, 2)}
FINE = ("x", "y", "c", "z")
ROWS_FIRST = (((0,), (0,)), ((), ()))
COLS_LAST = (((1,), (1,)), ((), ()))


def dot(a, b, dims=(((1,), (0,)), ((), ()))):
    return lax.dot_general(a, b, dims, preferred_element_type=jnp.float32)


def feature_map(value):
    return jnp.where(value > 0, value + 1.0, jnp.exp(jnp.minimum(value, 0.0)))


def same_head():
    row = lax.broadcasted_iota(jnp.int32, (D, D), 0) // DH
    col = lax.broadcasted_iota(jnp.int32, (D, D), 1) // DH
    return row == col


def alive_of(count_ref, rows):
    return (lax.broadcasted_iota(jnp.int32, (rows, 1), 0) < count_ref[...]).astype(jnp.float32)


def store_packed(out_ref, dense, vectors):
    kept = jnp.where(same_head(), dense, 0.0)
    folded = kept[0:DH]
    for h in range(1, HEADS):
        folded = folded + kept[h * DH : (h + 1) * DH]
    row = lax.broadcasted_iota(jnp.int32, (TILE, D), 0)
    last = jnp.zeros((TILE, D), jnp.float32)
    for i, vector in enumerate(vectors):
        last = jnp.where(row == i, vector, last)
    tiles = [folded[t * TILE : (t + 1) * TILE] for t in range(4)] + [last]
    for t, tile in enumerate(tiles):
        for r in range(TILE):
            out_ref[r, :, t * D : (t + 1) * D] = tile[r : r + 1]


def load_packed(packed_ref):
    tiles = [
        jnp.concatenate([packed_ref[r, :, t * D : (t + 1) * D] for r in range(TILE)], axis=0) for t in range(5)
    ]
    folded = jnp.concatenate(tiles[:4], axis=0)
    return jnp.where(same_head(), jnp.concatenate([folded] * HEADS, axis=0), 0.0), tiles[4]


def halves(value):
    high = value.astype(jnp.bfloat16)
    return high, (value - high.astype(jnp.float32)).astype(jnp.bfloat16)


def dot3(a, b, dims=(((1,), (0,)), ((), ()))):
    return dot(a[0], b[0], dims) + (dot(a[0], b[1], dims) + dot(a[1], b[0], dims))


def head_sums(value, heads):
    high, low = halves(value)
    return dot(high, heads) + dot(low, heads)


def key_kernel(
    count_ref, feats_hbm, w_hbm, send_hbm, packed_ref, before_ref, after_ref,
    feats_ref, w_ref, send_ref, sems,
):
    sources = [(feats_hbm, feats_ref), (w_hbm.at[pl.ds(1, 2)], w_ref), (send_hbm, send_ref)]
    copies = [pltpu.make_async_copy(*pair, sems.at[i]) for i, pair in enumerate(sources)]
    for copy in copies:
        copy.start()
    for copy in copies:
        copy.wait()
    feats = feats_ref[...]
    slot = lax.broadcasted_iota(jnp.int32, (feats.shape[0], send_ref.shape[2]), 0)
    for side, out in ((0, before_ref), (1, after_ref)):
        chosen = (slot == send_ref[0, side : side + 1, :]).astype(jnp.bfloat16)
        out[...] = dot(chosen, feats, ROWS_FIRST).astype(jnp.bfloat16)
    key_map = feature_map(dot(feats, w_ref[0]))
    value_rows = dot(feats, w_ref[1])
    key_map = key_map * alive_of(count_ref, feats.shape[0])
    kv = dot3(halves(key_map), halves(value_rows), ROWS_FIRST)
    live = jnp.broadcast_to(count_ref[...].astype(jnp.float32), (1, D))
    store_packed(packed_ref, kv, [jnp.sum(key_map, axis=0, keepdims=True), live])


def hit_kernel(nbr_ref, count_ref, hits_ref):
    wide, total = hits_ref.shape
    slots = nbr_ref.shape[0]
    sub = 32
    one, none = jnp.ones((sub, 128), jnp.bfloat16), jnp.zeros((sub, 128), jnp.bfloat16)
    for b in range(total // 128):
        at = slice(b * 128, (b + 1) * 128)
        slot = lax.broadcasted_iota(jnp.int32, (slots, 128), 0)
        named = jnp.where(slot < count_ref[:, at], nbr_ref[:, at], -1)
        rows = [jnp.broadcast_to(named[s : s + 1], (sub, 128)).astype(jnp.int16) for s in range(slots)]
        own = (lax.broadcasted_iota(jnp.int32, (sub, 128), 1) + b * 128).astype(jnp.int16)
        place0 = lax.broadcasted_iota(jnp.int32, (sub, 128), 0)

        def body(i, carry):
            first = pl.multiple_of(i * sub, sub)
            place = (place0 + first).astype(jnp.int16)
            hits = jnp.where(place == own, one, none)
            for s in range(slots):
                hits = hits + jnp.where(place == rows[s], one, none)
            hits_ref[pl.ds(first, sub), at] = hits
            return carry

        lax.fori_loop(0, wide // sub, body, 0)


def graph_kernel(hits_ref, feats_ref, left_ref, right_ref, wg_ref, w_ref, agg_ref, graph_ref, query_ref, key_ref, value_ref):
    total = feats_ref.shape[0]
    rim = left_ref.shape[0]
    summed = dot(hits_ref[:total, :], feats_ref[...], ROWS_FIRST)
    summed += dot(hits_ref[total : total + rim, :], left_ref[...], ROWS_FIRST)
    summed += dot(hits_ref[total + rim :, :], right_ref[...], ROWS_FIRST)
    named = dot(hits_ref[...], jnp.ones((total + 2 * rim, 128), jnp.bfloat16), ROWS_FIRST)
    agg = (summed / jnp.concatenate([named, named], axis=1)).astype(jnp.bfloat16)
    agg_ref[...] = agg
    graph_ref[...] = 0.5 * dot(agg, wg_ref[...])
    feats = feats_ref[...]
    query_ref[...] = feature_map(dot(feats, w_ref[0]))
    key_ref[...] = feature_map(dot(feats, w_ref[1]))
    value_ref[...] = dot(feats, w_ref[2])


def mix_kernel(
    count_ref, packed_ref, feats_ref, agg_ref, query_ref, value_ref, graph_ref, grad_ref, gain_ref,
    out_ref, dnum_ref, packed_out_ref, terms_ref, scale_ref,
):
    kv, vectors = load_packed(packed_ref)
    kv = halves(kv)
    ks, live = vectors[0:1], vectors[1:2]
    factor = 1.0 / (DH * live)
    scale_ref[...] = lax.rsqrt(live)
    heads = same_head().astype(jnp.bfloat16)
    gain_alive = gain_ref[...] * alive_of(count_ref, query_ref.shape[0])

    query_map = query_ref[...]
    query_halves = halves(query_map)
    numer = value_ref[...] + factor * dot3(query_halves, kv)
    denom = 1.0 + factor * head_sums(query_map * ks, heads)
    inverse = 1.0 / denom
    attn = numer * inverse
    mixed = 0.5 * attn + graph_ref[...]
    mean = jnp.sum(mixed, -1, keepdims=True) / D
    spread = jnp.sum(mixed * mixed, -1, keepdims=True) / D - mean * mean
    rstd = lax.rsqrt(spread + 1e-05)
    normed = (mixed - mean) * rstd
    out_ref[...] = (normed * gain_alive).astype(jnp.bfloat16)
    dnormed = grad_ref[...].astype(jnp.float32) * gain_alive
    dmixed = rstd * (
        dnormed
        - jnp.sum(dnormed, -1, keepdims=True) / D
        - normed * (jnp.sum(dnormed * normed, -1, keepdims=True) / D)
    )
    dattn = 0.5 * dmixed
    dnum = dattn * inverse
    dnum_ref[...] = dnum
    dden = -head_sums(dattn * attn, heads) * inverse
    dkv = dot3(query_halves, halves(dnum), ROWS_FIRST)
    dks = jnp.sum(query_map * dden, axis=0, keepdims=True)
    store_packed(packed_out_ref, factor * dkv, [factor * dks])
    terms_ref[0] = dot(agg_ref[...], dattn.astype(jnp.bfloat16), ROWS_FIRST)
    dquery = factor * (dot3(halves(dnum), kv, COLS_LAST) + dden * ks) * jnp.minimum(query_map, 1.0)
    terms_ref[1] = dot(feats_ref[...], dquery.astype(jnp.bfloat16), ROWS_FIRST)


def grad_kernel(count_ref, packed_ref, feats_ref, key_ref, value_ref, dnum_ref, held_ref, terms_ref):
    terms_ref[0] = held_ref[0]
    terms_ref[1] = held_ref[1]
    dkv, vectors = load_packed(packed_ref)
    dkv = halves(dkv)
    feats = feats_ref[...]
    alive = alive_of(count_ref, feats.shape[0])
    key_map = key_ref[...]
    slope = jnp.minimum(key_map, 1.0) * alive
    dvalue = dnum_ref[...] + dot3(halves(key_map * alive), dkv)
    dkey = (dot3(halves(value_ref[...]), dkv, COLS_LAST) + vectors[0:1]) * slope
    terms_ref[2] = dot(feats, dkey.astype(jnp.bfloat16), ROWS_FIRST)
    terms_ref[3] = dot(feats, dvalue.astype(jnp.bfloat16), ROWS_FIRST)


def split_kernel(total_ref, qkv_ref, graph_ref, sems):
    copies = [
        pltpu.make_async_copy(total_ref.at[pl.ds(1, 3)], qkv_ref, sems.at[0]),
        pltpu.make_async_copy(total_ref.at[0], graph_ref, sems.at[1]),
    ]
    for copy in copies:
        copy.start()
    for copy in copies:
        copy.wait()


def call(kernel, name, shapes, *args, away=(), outs_away=False, scratch=(), limit=VMEM_LIMIT):
    near = pl.BlockSpec(memory_space=pltpu.VMEM)
    far = pl.BlockSpec(memory_space=pltpu.MemorySpace.HBM)
    return pl.pallas_call(
        kernel,
        in_specs=[far if i in away else near for i in range(len(args))],
        out_specs=jax.tree.map(lambda one: far if outs_away else near, shapes),
        out_shape=shapes,
        scratch_shapes=scratch,
        cost_estimate=pl.CostEstimate(flops=10**9, bytes_accessed=10**7, transcendentals=0),
        compiler_params=pltpu.CompilerParams(vmem_limit_bytes=limit),
        name=name,
    )(*args)


def scatter_sum(value, axes, count):
    parts = lax.all_to_all(value, axes, 0, 0, tiled=True)
    return jnp.sum(parts.reshape(count, value.shape[0] // count, *value.shape[1:]), axis=0)


def gather(value, axes, count):
    copies = jnp.broadcast_to(value[None], (count, *value.shape)).reshape(count * value.shape[0], *value.shape[1:])
    return lax.all_to_all(copies, axes, 0, 0, tiled=True)


def gather_sum(value, axes, count):
    return jnp.sum(gather(value, axes, count).reshape(count, *value.shape), axis=0)


def sum_terms(terms, sizes, scale):
    value = scatter_sum(terms, "c", sizes["c"])
    value = scatter_sum(value, "x", sizes["x"])
    value = scatter_sum(value, "y", sizes["y"])
    value = gather_sum(value, "z", sizes["z"]) * scale
    value = gather(value, "y", sizes["y"])
    value = gather(value, "x", sizes["x"])
    return gather(value, "c", sizes["c"])


def local(sizes, node_feats, w_qkv, w_graph, ln_gain, out_grad, part_counts, send_rows, neighbours, neighbour_counts):
    rows = node_feats.shape[0]
    rim = send_rows.shape[2]
    near = sizes["x"] * sizes["c"]
    parts = near * sizes["y"] * sizes["z"]
    f32, bf16 = jnp.float32, jnp.bfloat16
    shape = jax.ShapeDtypeStruct
    count = part_counts.reshape(1, 1)
    rows_f32, rows_bf16 = shape((rows, D), f32), shape((rows, D), bf16)
    packed_shape, rim_shape = shape((TILE, 1, PACK), f32), shape((rim, D), bf16)
    together = lax.optimization_barrier

    packed, to_before, to_after = call(
        key_kernel, "keys", [packed_shape, rim_shape, rim_shape],
        count, node_feats, w_qkv, send_rows, away=(1, 2, 3), limit=None,
        scratch=[
            pltpu.VMEM((rows, D), bf16), pltpu.VMEM((2, D, D), bf16), pltpu.VMEM(send_rows.shape, jnp.int32),
            pltpu.SemaphoreType.DMA((3,)),
        ],
    )

    up = [(i, i + 1) for i in range(parts - 1)]
    down = [(j, i) for i, j in up]
    left = lax.ppermute(to_after, FINE, up)
    right = lax.ppermute(to_before, FINE, down)
    share = scatter_sum(packed, ("x", "c"), near)
    share, left, right = together((share, left, right))
    hits = call(
        hit_kernel, "hits", shape((rows + 2 * rim, rows), bf16), neighbours.T, neighbour_counts.reshape(1, rows)
    )
    agg, graph, query_map, key_map, value_rows = call(
        graph_kernel, "graph", [rows_bf16, rows_f32, rows_f32, rows_f32, rows_f32],
        hits, node_feats, left, right, w_graph, w_qkv,
    )
    share = gather_sum(share, "y", sizes["y"])
    share, agg, graph, query_map, key_map, value_rows = together((share, agg, graph, query_map, key_map, value_rows))
    share = gather_sum(share, "z", sizes["z"])
    packed = gather(share, ("x", "c"), near)

    node_out, dnum, dpacked, terms, scale = call(
        mix_kernel, "mix", [rows_bf16, rows_f32, packed_shape, shape((2, D, D), f32), shape((1, D), f32)],
        count, packed, node_feats, agg, query_map, value_rows, graph, out_grad, ln_gain.reshape(1, D),
    )

    share = scatter_sum(dpacked, ("x", "c"), near)
    share = gather_sum(share, "y", sizes["y"])
    share = gather_sum(share, "z", sizes["z"])
    dpacked = gather(share, ("x", "c"), near)

    terms = call(
        grad_kernel, "grads", shape((4, D, D), f32), count, dpacked, node_feats, key_map, value_rows, dnum, terms
    )
    total = sum_terms(terms.reshape(4 * D, D), sizes, scale).reshape(4, D, D)
    qkv_grad, graph_grad = call(
        split_kernel, "split", [shape((3, D, D), f32), shape((D, D), f32)], total,
        outs_away=True, scratch=[pltpu.SemaphoreType.DMA((2,))],
    )
    return node_out, qkv_grad, graph_grad


def solution(mesh):
    sizes = dict(zip(FINE, (*MESH_FACTORS[mesh.shape["dom"]], mesh.shape["head"])))
    fine = Mesh(mesh.devices.reshape(tuple(sizes.values())), FINE)
    return jax.shard_map(
        functools.partial(local, sizes),
        mesh=fine,
        in_specs=(
            P(FINE, None), P(), P(), P(), P(FINE, None), P(FINE), P(FINE, None, None), P(FINE, None), P(FINE),
        ),
        out_specs=(P(FINE, None), P(), P()),
        check_vma=False,
    )
```

```python
import functools

import jax
import jax.numpy as jnp
from jax import lax
from jax.experimental import pallas as pl
from jax.experimental.pallas import tpu as pltpu
from jax.sharding import Mesh, PartitionSpec as P

D = 256
DH = 32
HEADS = D // DH
TILE = 8
PACK = 5 * D
VMEM_LIMIT = 16 << 20
MESH_FACTORS = {64: (4, 8, 2), 8: (2, 2, 2)}
FINE = ("x", "y", "c", "z")
ROWS_FIRST = (((0,), (0,)), ((), ()))
COLS_LAST = (((1,), (1,)), ((), ()))


def dot(a, b, dims=(((1,), (0,)), ((), ()))):
    return lax.dot_general(a, b, dims, preferred_element_type=jnp.float32)


def feature_map(value):
    return jnp.where(value > 0, value + 1.0, jnp.exp(jnp.minimum(value, 0.0)))


def same_head():
    row = lax.broadcasted_iota(jnp.int32, (D, D), 0) // DH
    col = lax.broadcasted_iota(jnp.int32, (D, D), 1) // DH
    return row == col


def alive_of(count_ref, rows):
    return (lax.broadcasted_iota(jnp.int32, (rows, 1), 0) < count_ref[...]).astype(jnp.float32)


def store_packed(out_ref, dense, vectors):
    kept = jnp.where(same_head(), dense, 0.0)
    folded = kept[0:DH]
    for h in range(1, HEADS):
        folded = folded + kept[h * DH : (h + 1) * DH]
    row = lax.broadcasted_iota(jnp.int32, (TILE, D), 0)
    last = jnp.zeros((TILE, D), jnp.float32)
    for i, vector in enumerate(vectors):
        last = jnp.where(row == i, vector, last)
    tiles = [folded[t * TILE : (t + 1) * TILE] for t in range(4)] + [last]
    for t, tile in enumerate(tiles):
        for r in range(TILE):
            out_ref[r, :, t * D : (t + 1) * D] = tile[r : r + 1]


def load_packed(packed_ref):
    tiles = [
        jnp.concatenate([packed_ref[r, :, t * D : (t + 1) * D] for r in range(TILE)], axis=0) for t in range(5)
    ]
    folded = jnp.concatenate(tiles[:4], axis=0)
    return jnp.where(same_head(), jnp.concatenate([folded] * HEADS, axis=0), 0.0), tiles[4]


def halves(value):
    high = value.astype(jnp.bfloat16)
    return high, (value - high.astype(jnp.float32)).astype(jnp.bfloat16)


def dot3(a, b, dims=(((1,), (0,)), ((), ()))):
    return dot(a[0], b[0], dims) + (dot(a[0], b[1], dims) + dot(a[1], b[0], dims))


def head_sums(value, heads):
    high, low = halves(value)
    return dot(high, heads) + dot(low, heads)


def key_kernel(
    count_ref, feats_hbm, w_hbm, send_hbm, packed_ref, first_ref, second_ref,
    feats_ref, w_ref, send_ref, sems,
):
    sources = [(feats_hbm, feats_ref), (w_hbm.at[pl.ds(1, 2)], w_ref), (send_hbm, send_ref)]
    copies = [pltpu.make_async_copy(*pair, sems.at[i]) for i, pair in enumerate(sources)]
    for copy in copies:
        copy.start()
    for copy in copies:
        copy.wait()
    feats = feats_ref[...]
    slot = lax.broadcasted_iota(jnp.int32, (feats.shape[0], send_ref.shape[2]), 0)
    odd = lax.axis_index("z") % 2
    for turn, out in ((0, first_ref), (1, second_ref)):
        to_after = send_ref[0, 1:2, :] * (1 - odd) + send_ref[0, 0:1, :] * odd
        to_before = send_ref[0, 0:1, :] * (1 - odd) + send_ref[0, 1:2, :] * odd
        chosen = (slot == (to_before if turn else to_after)).astype(jnp.bfloat16)
        out[...] = dot(chosen, feats, ROWS_FIRST).astype(jnp.bfloat16)
    key_map = feature_map(dot(feats, w_ref[0]))
    value_rows = dot(feats, w_ref[1])
    key_map = key_map * alive_of(count_ref, feats.shape[0])
    kv = dot3(halves(key_map), halves(value_rows), ROWS_FIRST)
    live = jnp.broadcast_to(count_ref[...].astype(jnp.float32), (1, D))
    store_packed(packed_ref, kv, [jnp.sum(key_map, axis=0, keepdims=True), live])


def hit_kernel(nbr_ref, count_ref, hits_ref):
    wide, total = hits_ref.shape
    slots = nbr_ref.shape[0]
    sub = 32
    one, none = jnp.ones((sub, 128), jnp.bfloat16), jnp.zeros((sub, 128), jnp.bfloat16)
    for b in range(total // 128):
        at = slice(b * 128, (b + 1) * 128)
        slot = lax.broadcasted_iota(jnp.int32, (slots, 128), 0)
        named = jnp.where(slot < count_ref[:, at], nbr_ref[:, at], -1)
        rows = [jnp.broadcast_to(named[s : s + 1], (sub, 128)).astype(jnp.int16) for s in range(slots)]
        own = (lax.broadcasted_iota(jnp.int32, (sub, 128), 1) + b * 128).astype(jnp.int16)
        place0 = lax.broadcasted_iota(jnp.int32, (sub, 128), 0)

        def body(i, carry):
            first = pl.multiple_of(i * sub, sub)
            place = (place0 + first).astype(jnp.int16)
            hits = jnp.where(place == own, one, none)
            for s in range(slots):
                hits = hits + jnp.where(place == rows[s], one, none)
            hits_ref[pl.ds(first, sub), at] = hits
            return carry

        lax.fori_loop(0, wide // sub, body, 0)


def graph_kernel(hits_ref, feats_ref, first_ref, second_ref, grad_ref, gain_ref, held_ref, gain_out_ref):
    total = feats_ref.shape[0]
    rim = first_ref.shape[0]
    odd = lax.axis_index("z") % 2 == 1
    left = jnp.where(odd, first_ref[...], second_ref[...])
    right = jnp.where(odd, second_ref[...], first_ref[...])
    summed = dot(hits_ref[:total, :], feats_ref[...], ROWS_FIRST)
    summed += dot(hits_ref[total : total + rim, :], left, ROWS_FIRST)
    summed += dot(hits_ref[total + rim :, :], right, ROWS_FIRST)
    named = dot(hits_ref[...], jnp.ones((total + 2 * rim, 128), jnp.bfloat16), ROWS_FIRST)
    agg = (summed / jnp.concatenate([named, named], axis=1)).astype(jnp.bfloat16)
    held_ref[0] = agg
    held_ref[1] = grad_ref[...]
    gain_out_ref[...] = gain_ref[...]


def mix_kernel(
    count_ref, packed_ref, feats_ref, w_ref, wg_ref, held_ref, gain_ref,
    out_ref, dnum_ref, packed_out_ref, terms_ref, scale_ref,
):
    kv, vectors = load_packed(packed_ref)
    kv = halves(kv)
    ks, live = vectors[0:1], vectors[1:2]
    factor = 1.0 / (DH * live)
    scale_ref[...] = lax.rsqrt(live)
    heads = same_head().astype(jnp.bfloat16)
    gain_alive = gain_ref[...] * alive_of(count_ref, feats_ref.shape[0])

    feats, agg = feats_ref[...], held_ref[0]
    query_map = feature_map(dot(feats, w_ref[0]))
    query_halves = halves(query_map)
    numer = dot(feats, w_ref[2]) + factor * dot3(query_halves, kv)
    denom = 1.0 + factor * head_sums(query_map * ks, heads)
    inverse = 1.0 / denom
    attn = numer * inverse
    mixed = 0.5 * attn + 0.5 * dot(agg, wg_ref[...])
    mean = jnp.sum(mixed, -1, keepdims=True) / D
    spread = jnp.sum(mixed * mixed, -1, keepdims=True) / D - mean * mean
    rstd = lax.rsqrt(spread + 1e-05)
    normed = (mixed - mean) * rstd
    out_ref[...] = (normed * gain_alive).astype(jnp.bfloat16)
    dnormed = held_ref[1].astype(jnp.float32) * gain_alive
    dmixed = rstd * (
        dnormed
        - jnp.sum(dnormed, -1, keepdims=True) / D
        - normed * (jnp.sum(dnormed * normed, -1, keepdims=True) / D)
    )
    dattn = 0.5 * dmixed
    dnum = dattn * inverse
    dnum_ref[...] = dnum
    dden = -head_sums(dattn * attn, heads) * inverse
    dkv = dot3(query_halves, halves(dnum), ROWS_FIRST)
    dks = jnp.sum(query_map * dden, axis=0, keepdims=True)
    store_packed(packed_out_ref, factor * dkv, [factor * dks])
    terms_ref[0] = dot(agg, dattn.astype(jnp.bfloat16), ROWS_FIRST)
    dquery = factor * (dot3(halves(dnum), kv, COLS_LAST) + dden * ks) * jnp.minimum(query_map, 1.0)
    terms_ref[1] = dot(feats, dquery.astype(jnp.bfloat16), ROWS_FIRST)


def grad_kernel(count_ref, packed_ref, feats_ref, w_ref, dnum_ref, early_ref, terms_ref):
    terms_ref[0] = early_ref[0]
    terms_ref[1] = early_ref[1]
    dkv, vectors = load_packed(packed_ref)
    dkv = halves(dkv)
    feats = feats_ref[...]
    alive = alive_of(count_ref, feats.shape[0])
    key_map = feature_map(dot(feats, w_ref[1]))
    slope = jnp.minimum(key_map, 1.0) * alive
    dvalue = dnum_ref[...] + dot3(halves(key_map * alive), dkv)
    dkey = (dot3(halves(dot(feats, w_ref[2])), dkv, COLS_LAST) + vectors[0:1]) * slope
    terms_ref[2] = dot(feats, dkey.astype(jnp.bfloat16), ROWS_FIRST)
    terms_ref[3] = dot(feats, dvalue.astype(jnp.bfloat16), ROWS_FIRST)


def split_kernel(total_ref, qkv_ref, graph_ref, sems):
    copies = [
        pltpu.make_async_copy(total_ref.at[pl.ds(1, 3)], qkv_ref, sems.at[0]),
        pltpu.make_async_copy(total_ref.at[0], graph_ref, sems.at[1]),
    ]
    for copy in copies:
        copy.start()
    for copy in copies:
        copy.wait()


def call(kernel, name, shapes, *args, away=(), outs_away=False, scratch=(), limit=VMEM_LIMIT):
    near = pl.BlockSpec(memory_space=pltpu.VMEM)
    far = pl.BlockSpec(memory_space=pltpu.MemorySpace.HBM)
    return pl.pallas_call(
        kernel,
        in_specs=[far if i in away else near for i in range(len(args))],
        out_specs=jax.tree.map(lambda one: far if outs_away else near, shapes),
        out_shape=shapes,
        scratch_shapes=scratch,
        cost_estimate=pl.CostEstimate(flops=10**9, bytes_accessed=10**7, transcendentals=0),
        compiler_params=pltpu.CompilerParams(vmem_limit_bytes=limit),
        name=name,
    )(*args)


def scatter_sum(value, axes, count):
    parts = lax.all_to_all(value, axes, 0, 0, tiled=True)
    return jnp.sum(parts.reshape(count, value.shape[0] // count, *value.shape[1:]), axis=0)


def gather(value, axes, count):
    copies = jnp.broadcast_to(value[None], (count, *value.shape)).reshape(count * value.shape[0], *value.shape[1:])
    return lax.all_to_all(copies, axes, 0, 0, tiled=True)


def gather_sum(value, axes, count):
    return jnp.sum(gather(value, axes, count).reshape(count, *value.shape), axis=0)


def sum_terms(terms, sizes, scale):
    value = scatter_sum(terms, "c", sizes["c"])
    value = scatter_sum(value, "x", sizes["x"])
    value = scatter_sum(value, "y", sizes["y"])
    value = gather_sum(value, "z", sizes["z"]) * scale
    value = gather(value, "y", sizes["y"])
    value = gather(value, "x", sizes["x"])
    return gather(value, "c", sizes["c"])


def local(sizes, node_feats, w_qkv, w_graph, ln_gain, out_grad, part_counts, send_rows, neighbours, neighbour_counts):
    rows = node_feats.shape[0]
    rim = send_rows.shape[2]
    near = sizes["x"] * sizes["c"]
    parts = near * sizes["y"] * sizes["z"]
    f32, bf16 = jnp.float32, jnp.bfloat16
    shape = jax.ShapeDtypeStruct
    count = part_counts.reshape(1, 1)
    rows_f32, rows_bf16 = shape((rows, D), f32), shape((rows, D), bf16)
    packed_shape, rim_shape = shape((TILE, 1, PACK), f32), shape((rim, D), bf16)
    together = lax.optimization_barrier

    packed, first, second = call(
        key_kernel, "keys", [packed_shape, rim_shape, rim_shape],
        count, node_feats, w_qkv, send_rows, away=(1, 2, 3), limit=None,
        scratch=[
            pltpu.VMEM((rows, D), bf16), pltpu.VMEM((2, D, D), bf16), pltpu.VMEM(send_rows.shape, jnp.int32),
            pltpu.SemaphoreType.DMA((3,)),
        ],
    )

    swap = [(i, i ^ 1) for i in range(parts)]
    cross = [pair for i in range(1, parts - 1, 2) for pair in ((i, i + 1), (i + 1, i))]
    first = lax.ppermute(first, FINE, swap)
    second = lax.ppermute(second, FINE, cross)
    share = scatter_sum(packed, ("x", "c"), near)
    share, first, second, named = together((share, first, second, neighbours))
    hits = call(
        hit_kernel, "hits", shape((rows + 2 * rim, rows), bf16), named.T, neighbour_counts.reshape(1, rows)
    )
    held, gain = call(
        graph_kernel, "graph", [shape((2, rows, D), bf16), shape((1, D), f32)],
        hits, node_feats, first, second, out_grad, ln_gain.reshape(1, D),
    )
    share = gather_sum(share, "y", sizes["y"])
    share, held, gain = together((share, held, gain))
    share = gather_sum(share, "z", sizes["z"])
    packed = gather(share, ("x", "c"), near)

    node_out, dnum, dpacked, terms, scale = call(
        mix_kernel, "mix", [rows_bf16, rows_f32, packed_shape, shape((2, D, D), f32), shape((1, D), f32)],
        count, packed, node_feats, w_qkv, w_graph, held, gain,
    )

    share = scatter_sum(dpacked, ("x", "c"), near)
    share = gather_sum(share, "y", sizes["y"])
    share = gather_sum(share, "z", sizes["z"])
    dpacked = gather(share, ("x", "c"), near)

    terms = call(grad_kernel, "grads", shape((4, D, D), f32), count, dpacked, node_feats, w_qkv, dnum, terms)
    total = sum_terms(terms.reshape(4 * D, D), sizes, scale).reshape(4, D, D)
    qkv_grad, graph_grad = call(
        split_kernel, "split", [shape((3, D, D), f32), shape((D, D), f32)], total,
        outs_away=True, scratch=[pltpu.SemaphoreType.DMA((2,))],
    )
    return node_out, qkv_grad, graph_grad


def solution(mesh):
    sizes = dict(zip(FINE, (*MESH_FACTORS[mesh.shape["dom"]], mesh.shape["head"])))
    fine = Mesh(mesh.devices.reshape(tuple(sizes.values())), FINE)
    return jax.shard_map(
        functools.partial(local, sizes),
        mesh=fine,
        in_specs=(
            P(FINE, None), P(), P(), P(), P(FINE, None), P(FINE), P(FINE, None, None), P(FINE, None), P(FINE),
        ),
        out_specs=(P(FINE, None), P(), P()),
        check_vma=False,
    )
```

```python
import functools

import jax
import jax.numpy as jnp
from jax import lax
from jax.experimental import pallas as pl
from jax.experimental.pallas import tpu as pltpu
from jax.sharding import Mesh, PartitionSpec as P


D = 256
DH = 32
HEADS = D // DH
TILE = 8
PACK = 5 * D
VMEM_LIMIT = 16 << 20
MESH_FACTORS = {64: (4, 8, 2), 8: (2, 2, 2)}
FINE = ("x", "y", "c", "z")
ROWS_FIRST = (((0,), (0,)), ((), ()))
COLS_LAST = (((1,), (1,)), ((), ()))


def dot(a, b, dims=(((1,), (0,)), ((), ()))):
    return lax.dot_general(a, b, dims, preferred_element_type=jnp.float32)


def feature_map(value):
    return jnp.where(value > 0, value + 1.0, jnp.exp(jnp.minimum(value, 0.0)))


def same_head():
    row = lax.broadcasted_iota(jnp.int32, (D, D), 0) // DH
    col = lax.broadcasted_iota(jnp.int32, (D, D), 1) // DH
    return row == col


def alive_of(count_ref, rows):
    return (lax.broadcasted_iota(jnp.int32, (rows, 1), 0) < count_ref[...]).astype(jnp.float32)


def store_packed(out_ref, dense, vectors):
    kept = jnp.where(same_head(), dense, 0.0)
    folded = kept[0:DH]
    for h in range(1, HEADS):
        folded = folded + kept[h * DH : (h + 1) * DH]
    row = lax.broadcasted_iota(jnp.int32, (TILE, D), 0)
    last = jnp.zeros((TILE, D), jnp.float32)
    for i, vector in enumerate(vectors):
        last = jnp.where(row == i, vector, last)
    tiles = [folded[t * TILE : (t + 1) * TILE] for t in range(4)] + [last]
    for t, tile in enumerate(tiles):
        for r in range(TILE):
            out_ref[r, :, t * D : (t + 1) * D] = tile[r : r + 1]


def load_packed(packed_ref):
    tiles = [
        jnp.concatenate([packed_ref[r, :, t * D : (t + 1) * D] for r in range(TILE)], axis=0) for t in range(5)
    ]
    folded = jnp.concatenate(tiles[:4], axis=0)
    return jnp.where(same_head(), jnp.concatenate([folded] * HEADS, axis=0), 0.0), tiles[4]


def halves(value):
    high = value.astype(jnp.bfloat16)
    return high, (value - high.astype(jnp.float32)).astype(jnp.bfloat16)


def dot3(a, b, dims=(((1,), (0,)), ((), ()))):
    return dot(a[0], b[0], dims) + (dot(a[0], b[1], dims) + dot(a[1], b[0], dims))


def head_sums(value, heads):
    high, low = halves(value)
    return dot(high, heads) + dot(low, heads)


def key_kernel(
    count_ref, feats_hbm, w_hbm, send_hbm, packed_ref, first_ref, second_ref,
    feats_ref, w_ref, send_ref, sems,
):
    sources = [(feats_hbm, feats_ref), (w_hbm.at[pl.ds(1, 2)], w_ref), (send_hbm, send_ref)]
    copies = [pltpu.make_async_copy(*pair, sems.at[i]) for i, pair in enumerate(sources)]
    for copy in copies:
        copy.start()
    for copy in copies:
        copy.wait()
    feats = feats_ref[...]
    slot = lax.broadcasted_iota(jnp.int32, (feats.shape[0], send_ref.shape[2]), 0)
    odd = lax.axis_index("z") % 2
    for turn, out in ((0, first_ref), (1, second_ref)):
        to_after = send_ref[0, 1:2, :] * (1 - odd) + send_ref[0, 0:1, :] * odd
        to_before = send_ref[0, 0:1, :] * (1 - odd) + send_ref[0, 1:2, :] * odd
        chosen = (slot == (to_before if turn else to_after)).astype(jnp.bfloat16)
        out[...] = dot(chosen, feats, ROWS_FIRST).astype(jnp.bfloat16)
    key_map = feature_map(dot(feats, w_ref[0]))
    value_rows = dot(feats, w_ref[1])
    key_map = key_map * alive_of(count_ref, feats.shape[0])
    kv = dot3(halves(key_map), halves(value_rows), ROWS_FIRST)
    live = jnp.broadcast_to(count_ref[...].astype(jnp.float32), (1, D))
    store_packed(packed_ref, kv, [jnp.sum(key_map, axis=0, keepdims=True), live])


def hit_kernel(nbr_ref, count_ref, hits_ref):
    wide, total = hits_ref.shape
    slots = nbr_ref.shape[0]
    sub = 32
    one, none = jnp.ones((sub, 128), jnp.bfloat16), jnp.zeros((sub, 128), jnp.bfloat16)
    for b in range(total // 128):
        at = slice(b * 128, (b + 1) * 128)
        slot = lax.broadcasted_iota(jnp.int32, (slots, 128), 0)
        named = jnp.where(slot < count_ref[:, at], nbr_ref[:, at], -1)
        rows = [jnp.broadcast_to(named[s : s + 1], (sub, 128)).astype(jnp.int16) for s in range(slots)]
        own = (lax.broadcasted_iota(jnp.int32, (sub, 128), 1) + b * 128).astype(jnp.int16)
        place0 = lax.broadcasted_iota(jnp.int32, (sub, 128), 0)

        def body(i, carry):
            first = pl.multiple_of(i * sub, sub)
            place = (place0 + first).astype(jnp.int16)
            hits = jnp.where(place == own, one, none)
            for s in range(slots):
                hits = hits + jnp.where(place == rows[s], one, none)
            hits_ref[pl.ds(first, sub), at] = hits
            return carry

        lax.fori_loop(0, wide // sub, body, 0)


def graph_kernel(hits_ref, feats_ref, first_ref, second_ref, grad_ref, gain_ref, held_ref, gain_out_ref):
    total = feats_ref.shape[0]
    rim = first_ref.shape[0]
    odd = lax.axis_index("z") % 2 == 1
    left = jnp.where(odd, first_ref[...], second_ref[...])
    right = jnp.where(odd, second_ref[...], first_ref[...])
    summed = dot(hits_ref[:total, :], feats_ref[...], ROWS_FIRST)
    summed += dot(hits_ref[total : total + rim, :], left, ROWS_FIRST)
    summed += dot(hits_ref[total + rim :, :], right, ROWS_FIRST)
    named = dot(hits_ref[...], jnp.ones((total + 2 * rim, 128), jnp.bfloat16), ROWS_FIRST)
    agg = (summed / jnp.concatenate([named, named], axis=1)).astype(jnp.bfloat16)
    held_ref[0] = agg
    held_ref[1] = grad_ref[...]
    gain_out_ref[...] = gain_ref[...]


def mix_kernel(
    count_ref, packed_ref, feats_ref, w_ref, wg_ref, held_ref, gain_ref,
    out_ref, dnum_ref, packed_out_ref, terms_ref, scale_ref,
):
    kv, vectors = load_packed(packed_ref)
    kv = halves(kv)
    ks, live = vectors[0:1], vectors[1:2]
    factor = 1.0 / (DH * live)
    scale_ref[...] = lax.rsqrt(live)
    heads = same_head().astype(jnp.bfloat16)
    gain_alive = gain_ref[...] * alive_of(count_ref, feats_ref.shape[0])

    feats, agg = feats_ref[...], held_ref[0]
    query_map = feature_map(dot(feats, w_ref[0]))
    query_halves = halves(query_map)
    numer = dot(feats, w_ref[2]) + factor * dot3(query_halves, kv)
    denom = 1.0 + factor * head_sums(query_map * ks, heads)
    inverse = 1.0 / denom
    attn = numer * inverse
    mixed = 0.5 * attn + 0.5 * dot(agg, wg_ref[...])
    mean = jnp.sum(mixed, -1, keepdims=True) / D
    spread = jnp.sum(mixed * mixed, -1, keepdims=True) / D - mean * mean
    rstd = lax.rsqrt(spread + 1e-05)
    normed = (mixed - mean) * rstd
    out_ref[...] = (normed * gain_alive).astype(jnp.bfloat16)
    dnormed = held_ref[1].astype(jnp.float32) * gain_alive
    dmixed = rstd * (
        dnormed
        - jnp.sum(dnormed, -1, keepdims=True) / D
        - normed * (jnp.sum(dnormed * normed, -1, keepdims=True) / D)
    )
    dattn = 0.5 * dmixed
    dnum = dattn * inverse
    dnum_ref[...] = dnum
    dden = -head_sums(dattn * attn, heads) * inverse
    dkv = dot3(query_halves, halves(dnum), ROWS_FIRST)
    dks = jnp.sum(query_map * dden, axis=0, keepdims=True)
    store_packed(packed_out_ref, factor * dkv, [factor * dks])
    terms_ref[0] = dot(agg, dattn.astype(jnp.bfloat16), ROWS_FIRST)
    dquery = factor * (dot3(halves(dnum), kv, COLS_LAST) + dden * ks) * jnp.minimum(query_map, 1.0)
    terms_ref[1] = dot(feats, dquery.astype(jnp.bfloat16), ROWS_FIRST)


def grad_kernel(count_ref, packed_ref, feats_ref, w_ref, dnum_ref, early_ref, terms_ref):
    terms_ref[0] = early_ref[0]
    terms_ref[1] = early_ref[1]
    dkv, vectors = load_packed(packed_ref)
    dkv = halves(dkv)
    feats = feats_ref[...]
    alive = alive_of(count_ref, feats.shape[0])
    key_map = feature_map(dot(feats, w_ref[1]))
    slope = jnp.minimum(key_map, 1.0) * alive
    dvalue = dnum_ref[...] + dot3(halves(key_map * alive), dkv)
    dkey = (dot3(halves(dot(feats, w_ref[2])), dkv, COLS_LAST) + vectors[0:1]) * slope
    terms_ref[2] = dot(feats, dkey.astype(jnp.bfloat16), ROWS_FIRST)
    terms_ref[3] = dot(feats, dvalue.astype(jnp.bfloat16), ROWS_FIRST)


def split_kernel(total_ref, qkv_ref, graph_ref, sems):
    copies = [
        pltpu.make_async_copy(total_ref.at[pl.ds(1, 3)], qkv_ref, sems.at[0]),
        pltpu.make_async_copy(total_ref.at[0], graph_ref, sems.at[1]),
    ]
    for copy in copies:
        copy.start()
    for copy in copies:
        copy.wait()


def call(kernel, shapes, *args, away=(), outs_away=False, scratch=(), limit=VMEM_LIMIT):
    near = pl.BlockSpec(memory_space=pltpu.VMEM)
    far = pl.BlockSpec(memory_space=pltpu.MemorySpace.HBM)
    return pl.pallas_call(
        kernel,
        in_specs=[far if i in away else near for i in range(len(args))],
        out_specs=jax.tree.map(lambda one: far if outs_away else near, shapes),
        out_shape=shapes,
        scratch_shapes=scratch,
        cost_estimate=pl.CostEstimate(flops=10**9, bytes_accessed=10**7, transcendentals=0),
        compiler_params=pltpu.CompilerParams(vmem_limit_bytes=limit),
    )(*args)


def scatter_sum(value, axes, count):
    parts = lax.all_to_all(value, axes, 0, 0, tiled=True)
    return jnp.sum(parts.reshape(count, value.shape[0] // count, *value.shape[1:]), axis=0)


def gather(value, axes, count):
    copies = jnp.broadcast_to(value[None], (count, *value.shape)).reshape(count * value.shape[0], *value.shape[1:])
    return lax.all_to_all(copies, axes, 0, 0, tiled=True)


def gather_sum(value, axes, count):
    return jnp.sum(gather(value, axes, count).reshape(count, *value.shape), axis=0)


def sum_terms(terms, sizes, scale):
    value = scatter_sum(terms, "c", sizes["c"])
    value = scatter_sum(value, "x", sizes["x"])
    value = scatter_sum(value, "y", sizes["y"])
    value = gather_sum(value, "z", sizes["z"]) * scale
    value = gather(value, "y", sizes["y"])
    value = gather(value, "x", sizes["x"])
    return gather(value, "c", sizes["c"])


def local(sizes, node_feats, w_qkv, w_graph, ln_gain, out_grad, part_counts, send_rows, neighbours, neighbour_counts):
    rows = node_feats.shape[0]
    rim = send_rows.shape[2]
    near = sizes["x"] * sizes["c"]
    parts = near * sizes["y"] * sizes["z"]
    f32, bf16 = jnp.float32, jnp.bfloat16
    shape = jax.ShapeDtypeStruct
    count = part_counts.reshape(1, 1)
    rows_f32, rows_bf16 = shape((rows, D), f32), shape((rows, D), bf16)
    packed_shape, rim_shape = shape((TILE, 1, PACK), f32), shape((rim, D), bf16)
    together = lax.optimization_barrier

    packed, first, second = call(
        key_kernel, [packed_shape, rim_shape, rim_shape],
        count, node_feats, w_qkv, send_rows, away=(1, 2, 3), limit=None,
        scratch=[
            pltpu.VMEM((rows, D), bf16), pltpu.VMEM((2, D, D), bf16), pltpu.VMEM(send_rows.shape, jnp.int32),
            pltpu.SemaphoreType.DMA((3,)),
        ],
    )

    swap = [(i, i ^ 1) for i in range(parts)]
    cross = [pair for i in range(1, parts - 1, 2) for pair in ((i, i + 1), (i + 1, i))]
    first = lax.ppermute(first, FINE, swap)
    second = lax.ppermute(second, FINE, cross)
    share = scatter_sum(packed, ("x", "c"), near)
    share, named = together((share, neighbours))
    hits = call(hit_kernel, shape((rows + 2 * rim, rows), bf16), named.T, neighbour_counts.reshape(1, rows))
    held, gain = call(
        graph_kernel, [shape((2, rows, D), bf16), shape((1, D), f32)],
        hits, node_feats, first, second, out_grad, ln_gain.reshape(1, D),
    )
    share = gather_sum(share, "y", sizes["y"])
    share, held, gain = together((share, held, gain))
    share = gather_sum(share, "z", sizes["z"])
    packed = gather(share, ("x", "c"), near)

    node_out, dnum, dpacked, terms, scale = call(
        mix_kernel, [rows_bf16, rows_f32, packed_shape, shape((2, D, D), f32), shape((1, D), f32)],
        count, packed, node_feats, w_qkv, w_graph, held, gain,
    )

    share = scatter_sum(dpacked, ("x", "c"), near)
    share = gather_sum(share, "y", sizes["y"])
    share = gather_sum(share, "z", sizes["z"])
    dpacked = gather(share, ("x", "c"), near)

    terms = call(grad_kernel, shape((4, D, D), f32), count, dpacked, node_feats, w_qkv, dnum, terms)
    total = sum_terms(terms.reshape(4 * D, D), sizes, scale).reshape(4, D, D)
    qkv_grad, graph_grad = call(
        split_kernel, [shape((3, D, D), f32), shape((D, D), f32)], total,
        outs_away=True, scratch=[pltpu.SemaphoreType.DMA((2,))],
    )
    return node_out, qkv_grad, graph_grad


def solution(mesh):
    sizes = dict(zip(FINE, (*MESH_FACTORS[mesh.shape["dom"]], mesh.shape["head"])))
    fine = Mesh(mesh.devices.reshape(tuple(sizes.values())), FINE)
    return jax.shard_map(
        functools.partial(local, sizes),
        mesh=fine,
        in_specs=(
            P(FINE, None), P(), P(), P(), P(FINE, None), P(FINE), P(FINE, None, None), P(FINE, None), P(FINE),
        ),
        out_specs=(P(FINE, None), P(), P()),
        check_vma=False,
    )
```

```python
import functools

import jax
import jax.numpy as jnp
from jax import lax
from jax.experimental import pallas as pl
from jax.experimental.pallas import tpu as pltpu
from jax.sharding import Mesh, PartitionSpec as P


D = 256
DH = 32
HEADS = D // DH
TILE = 8
PACK = 5 * D
VMEM_LIMIT = 16 << 20
MESH_FACTORS = {64: (4, 8, 2), 8: (2, 2, 2)}
FINE = ("x", "y", "c", "z")
ROWS_FIRST = (((0,), (0,)), ((), ()))
COLS_LAST = (((1,), (1,)), ((), ()))


def dot(a, b, dims=(((1,), (0,)), ((), ()))):
    return lax.dot_general(a, b, dims, preferred_element_type=jnp.float32)


def feature_map(value):
    return jnp.where(value > 0, value + 1.0, jnp.exp(jnp.minimum(value, 0.0)))


def same_head():
    row = lax.broadcasted_iota(jnp.int32, (D, D), 0) // DH
    col = lax.broadcasted_iota(jnp.int32, (D, D), 1) // DH
    return row == col


def alive_of(count_ref, rows):
    return (lax.broadcasted_iota(jnp.int32, (rows, 1), 0) < count_ref[...]).astype(jnp.float32)


def store_packed(out_ref, dense, vectors):
    kept = jnp.where(same_head(), dense, 0.0)
    folded = kept[0:DH]
    for h in range(1, HEADS):
        folded = folded + kept[h * DH : (h + 1) * DH]
    row = lax.broadcasted_iota(jnp.int32, (TILE, D), 0)
    last = jnp.zeros((TILE, D), jnp.float32)
    for i, vector in enumerate(vectors):
        last = jnp.where(row == i, vector, last)
    tiles = [folded[t * TILE : (t + 1) * TILE] for t in range(4)] + [last]
    for t, tile in enumerate(tiles):
        for r in range(TILE):
            out_ref[r, :, t * D : (t + 1) * D] = tile[r : r + 1]


def load_packed(packed_ref):
    tiles = [
        jnp.concatenate([packed_ref[r, :, t * D : (t + 1) * D] for r in range(TILE)], axis=0) for t in range(5)
    ]
    folded = jnp.concatenate(tiles[:4], axis=0)
    return jnp.where(same_head(), jnp.concatenate([folded] * HEADS, axis=0), 0.0), tiles[4]


def halves(value):
    high = value.astype(jnp.bfloat16)
    return high, (value - high.astype(jnp.float32)).astype(jnp.bfloat16)


def dot3(a, b, dims=(((1,), (0,)), ((), ()))):
    return dot(a[0], b[0], dims) + (dot(a[0], b[1], dims) + dot(a[1], b[0], dims))


def head_sums(value, heads):
    high, low = halves(value)
    return dot(high, heads) + dot(low, heads)


def key_kernel(
    count_ref, feats_hbm, w_hbm, send_hbm, packed_ref, first_ref, second_ref,
    feats_ref, w_ref, send_ref, sems,
):
    sources = [(feats_hbm, feats_ref), (w_hbm.at[pl.ds(1, 2)], w_ref), (send_hbm, send_ref)]
    copies = [pltpu.make_async_copy(*pair, sems.at[i]) for i, pair in enumerate(sources)]
    for copy in copies:
        copy.start()
    for copy in copies:
        copy.wait()
    feats = feats_ref[...]
    slot = lax.broadcasted_iota(jnp.int32, (feats.shape[0], send_ref.shape[2]), 0)
    odd = lax.axis_index("z") % 2
    for turn, out in ((0, first_ref), (1, second_ref)):
        to_after = send_ref[0, 1:2, :] * (1 - odd) + send_ref[0, 0:1, :] * odd
        to_before = send_ref[0, 0:1, :] * (1 - odd) + send_ref[0, 1:2, :] * odd
        chosen = (slot == (to_before if turn else to_after)).astype(jnp.bfloat16)
        out[...] = dot(chosen, feats, ROWS_FIRST).astype(jnp.bfloat16)
    key_map = feature_map(dot(feats, w_ref[0]))
    value_rows = dot(feats, w_ref[1])
    key_map = key_map * alive_of(count_ref, feats.shape[0])
    kv = dot3(halves(key_map), halves(value_rows), ROWS_FIRST)
    live = jnp.broadcast_to(count_ref[...].astype(jnp.float32), (1, D))
    store_packed(packed_ref, kv, [jnp.sum(key_map, axis=0, keepdims=True), live])


def hit_kernel(nbr_ref, count_ref, hits_ref):
    wide, total = hits_ref.shape
    slots = nbr_ref.shape[0]
    sub = 32
    one, none = jnp.ones((sub, 128), jnp.bfloat16), jnp.zeros((sub, 128), jnp.bfloat16)
    for b in range(total // 128):
        at = slice(b * 128, (b + 1) * 128)
        slot = lax.broadcasted_iota(jnp.int32, (slots, 128), 0)
        named = jnp.where(slot < count_ref[:, at], nbr_ref[:, at], -1)
        rows = [jnp.broadcast_to(named[s : s + 1], (sub, 128)).astype(jnp.int16) for s in range(slots)]
        own = (lax.broadcasted_iota(jnp.int32, (sub, 128), 1) + b * 128).astype(jnp.int16)
        place0 = lax.broadcasted_iota(jnp.int32, (sub, 128), 0)

        def body(i, carry):
            first = pl.multiple_of(i * sub, sub)
            place = (place0 + first).astype(jnp.int16)
            hits = jnp.where(place == own, one, none)
            for s in range(slots):
                hits = hits + jnp.where(place == rows[s], one, none)
            hits_ref[pl.ds(first, sub), at] = hits
            return carry

        lax.fori_loop(0, wide // sub, body, 0)


def graph_kernel(hits_ref, feats_ref, first_ref, second_ref, grad_ref, gain_ref, held_ref, gain_out_ref):
    total = feats_ref.shape[0]
    rim = first_ref.shape[0]
    odd = lax.axis_index("z") % 2 == 1
    left = jnp.where(odd, first_ref[...], second_ref[...])
    right = jnp.where(odd, second_ref[...], first_ref[...])
    summed = dot(hits_ref[:total, :], feats_ref[...], ROWS_FIRST)
    summed += dot(hits_ref[total : total + rim, :], left, ROWS_FIRST)
    summed += dot(hits_ref[total + rim :, :], right, ROWS_FIRST)
    named = dot(hits_ref[...], jnp.ones((total + 2 * rim, 128), jnp.bfloat16), ROWS_FIRST)
    agg = (summed / jnp.concatenate([named, named], axis=1)).astype(jnp.bfloat16)
    held_ref[0] = agg
    held_ref[1] = grad_ref[...]
    gain_out_ref[...] = gain_ref[...]


def mix_kernel(
    count_ref, packed_ref, feats_ref, w_ref, wg_ref, held_ref, gain_ref,
    out_ref, dnum_ref, packed_out_ref, terms_ref, scale_ref,
):
    kv, vectors = load_packed(packed_ref)
    kv = halves(kv)
    ks, live = vectors[0:1], vectors[1:2]
    factor = 1.0 / (DH * live)
    scale_ref[...] = lax.rsqrt(live)
    heads = same_head().astype(jnp.bfloat16)
    gain_alive = gain_ref[...] * alive_of(count_ref, feats_ref.shape[0])

    feats, agg = feats_ref[...], held_ref[0]
    query_map = feature_map(dot(feats, w_ref[0]))
    query_halves = halves(query_map)
    numer = dot(feats, w_ref[2]) + factor * dot3(query_halves, kv)
    denom = 1.0 + factor * head_sums(query_map * ks, heads)
    inverse = 1.0 / denom
    attn = numer * inverse
    mixed = 0.5 * attn + 0.5 * dot(agg, wg_ref[...])
    mean = jnp.sum(mixed, -1, keepdims=True) / D
    spread = jnp.sum(mixed * mixed, -1, keepdims=True) / D - mean * mean
    rstd = lax.rsqrt(spread + 1e-05)
    normed = (mixed - mean) * rstd
    out_ref[...] = (normed * gain_alive).astype(jnp.bfloat16)
    dnormed = held_ref[1].astype(jnp.float32) * gain_alive
    dmixed = rstd * (
        dnormed
        - jnp.sum(dnormed, -1, keepdims=True) / D
        - normed * (jnp.sum(dnormed * normed, -1, keepdims=True) / D)
    )
    dattn = 0.5 * dmixed
    dnum = dattn * inverse
    dnum_ref[...] = dnum
    dden = -head_sums(dattn * attn, heads) * inverse
    dkv = dot3(query_halves, halves(dnum), ROWS_FIRST)
    dks = jnp.sum(query_map * dden, axis=0, keepdims=True)
    store_packed(packed_out_ref, factor * dkv, [factor * dks])
    terms_ref[0] = dot(agg, dattn.astype(jnp.bfloat16), ROWS_FIRST)
    dquery = factor * (dot3(halves(dnum), kv, COLS_LAST) + dden * ks) * jnp.minimum(query_map, 1.0)
    terms_ref[1] = dot(feats, dquery.astype(jnp.bfloat16), ROWS_FIRST)


def grad_kernel(count_ref, packed_ref, feats_ref, w_ref, dnum_ref, early_ref, terms_ref):
    terms_ref[0] = early_ref[0]
    terms_ref[1] = early_ref[1]
    dkv, vectors = load_packed(packed_ref)
    dkv = halves(dkv)
    feats = feats_ref[...]
    alive = alive_of(count_ref, feats.shape[0])
    key_map = feature_map(dot(feats, w_ref[1]))
    slope = jnp.minimum(key_map, 1.0) * alive
    dvalue = dnum_ref[...] + dot3(halves(key_map * alive), dkv)
    dkey = (dot3(halves(dot(feats, w_ref[2])), dkv, COLS_LAST) + vectors[0:1]) * slope
    terms_ref[2] = dot(feats, dkey.astype(jnp.bfloat16), ROWS_FIRST)
    terms_ref[3] = dot(feats, dvalue.astype(jnp.bfloat16), ROWS_FIRST)


def split_kernel(total_ref, qkv_ref, graph_ref, sems):
    copies = [
        pltpu.make_async_copy(total_ref.at[pl.ds(1, 3)], qkv_ref, sems.at[0]),
        pltpu.make_async_copy(total_ref.at[0], graph_ref, sems.at[1]),
    ]
    for copy in copies:
        copy.start()
    for copy in copies:
        copy.wait()


def call(kernel, shapes, *args, away=(), outs_away=False, scratch=(), limit=VMEM_LIMIT):
    near = pl.BlockSpec(memory_space=pltpu.VMEM)
    far = pl.BlockSpec(memory_space=pltpu.MemorySpace.HBM)
    return pl.pallas_call(
        kernel,
        in_specs=[far if i in away else near for i in range(len(args))],
        out_specs=jax.tree.map(lambda one: far if outs_away else near, shapes),
        out_shape=shapes,
        scratch_shapes=scratch,
        cost_estimate=pl.CostEstimate(flops=10**9, bytes_accessed=10**7, transcendentals=0),
        compiler_params=pltpu.CompilerParams(vmem_limit_bytes=limit),
    )(*args)


def scatter_sum(value, axes, count):
    parts = lax.all_to_all(value, axes, 0, 0, tiled=True)
    return jnp.sum(parts.reshape(count, value.shape[0] // count, *value.shape[1:]), axis=0)


def gather(value, axes, count):
    copies = jnp.broadcast_to(value[None], (count, *value.shape)).reshape(count * value.shape[0], *value.shape[1:])
    return lax.all_to_all(copies, axes, 0, 0, tiled=True)


def gather_sum(value, axes, count):
    return jnp.sum(gather(value, axes, count).reshape(count, *value.shape), axis=0)


def sum_terms(terms, sizes, scale):
    plane = ("x", "z")
    spread = sizes["x"] * sizes["z"]
    value = scatter_sum(terms, "c", sizes["c"])
    value = scatter_sum(value, plane, spread)
    value = gather_sum(value, "y", sizes["y"]) * scale
    value = gather(value, plane, spread)
    return gather(value, "c", sizes["c"])


def local(sizes, node_feats, w_qkv, w_graph, ln_gain, out_grad, part_counts, send_rows, neighbours, neighbour_counts):
    rows = node_feats.shape[0]
    rim = send_rows.shape[2]
    near = sizes["x"] * sizes["c"]
    parts = near * sizes["y"] * sizes["z"]
    f32, bf16 = jnp.float32, jnp.bfloat16
    shape = jax.ShapeDtypeStruct
    count = part_counts.reshape(1, 1)
    rows_f32, rows_bf16 = shape((rows, D), f32), shape((rows, D), bf16)
    packed_shape, rim_shape = shape((TILE, 1, PACK), f32), shape((rim, D), bf16)
    together = lax.optimization_barrier

    packed, first, second = call(
        key_kernel, [packed_shape, rim_shape, rim_shape],
        count, node_feats, w_qkv, send_rows, away=(1, 2, 3), limit=None,
        scratch=[
            pltpu.VMEM((rows, D), bf16), pltpu.VMEM((2, D, D), bf16), pltpu.VMEM(send_rows.shape, jnp.int32),
            pltpu.SemaphoreType.DMA((3,)),
        ],
    )

    swap = [(i, i ^ 1) for i in range(parts)]
    cross = [pair for i in range(1, parts - 1, 2) for pair in ((i, i + 1), (i + 1, i))]
    first = lax.ppermute(first, FINE, swap)
    second = lax.ppermute(second, FINE, cross)
    share = scatter_sum(packed, ("x", "c"), near)
    share, named = together((share, neighbours))
    hits = call(hit_kernel, shape((rows + 2 * rim, rows), bf16), named.T, neighbour_counts.reshape(1, rows))
    held, gain = call(
        graph_kernel, [shape((2, rows, D), bf16), shape((1, D), f32)],
        hits, node_feats, first, second, out_grad, ln_gain.reshape(1, D),
    )
    share = gather_sum(share, "y", sizes["y"])
    share, held, gain = together((share, held, gain))
    share = gather_sum(share, "z", sizes["z"])
    packed = gather(share, ("x", "c"), near)

    node_out, dnum, dpacked, terms, scale = call(
        mix_kernel, [rows_bf16, rows_f32, packed_shape, shape((2, D, D), f32), shape((1, D), f32)],
        count, packed, node_feats, w_qkv, w_graph, held, gain,
    )

    share = scatter_sum(dpacked, ("x", "c"), near)
    share = gather_sum(share, "y", sizes["y"])
    share = gather_sum(share, "z", sizes["z"])
    dpacked = gather(share, ("x", "c"), near)

    terms = call(grad_kernel, shape((4, D, D), f32), count, dpacked, node_feats, w_qkv, dnum, terms)
    total = sum_terms(terms.reshape(4 * D, D), sizes, scale).reshape(4, D, D)
    qkv_grad, graph_grad = call(
        split_kernel, [shape((3, D, D), f32), shape((D, D), f32)], total,
        outs_away=True, scratch=[pltpu.SemaphoreType.DMA((2,))],
    )
    return node_out, qkv_grad, graph_grad


def solution(mesh):
    sizes = dict(zip(FINE, (*MESH_FACTORS[mesh.shape["dom"]], mesh.shape["head"])))
    fine = Mesh(mesh.devices.reshape(tuple(sizes.values())), FINE)
    return jax.shard_map(
        functools.partial(local, sizes),
        mesh=fine,
        in_specs=(
            P(FINE, None), P(), P(), P(), P(FINE, None), P(FINE), P(FINE, None, None), P(FINE, None), P(FINE),
        ),
        out_specs=(P(FINE, None), P(), P()),
        check_vma=False,
    )
```

```python
import functools

import jax
import jax.numpy as jnp
from jax import lax
from jax.experimental import pallas as pl
from jax.experimental.pallas import tpu as pltpu
from jax.sharding import Mesh, PartitionSpec as P


D = 256
DH = 32
HEADS = D // DH
TILE = 8
PACK = 5 * D
VMEM_LIMIT = 16 << 20
MESH_FACTORS = {64: (4, 8, 2), 8: (2, 2, 2)}
FINE = ("x", "y", "c", "z")
ROWS_FIRST = (((0,), (0,)), ((), ()))
COLS_LAST = (((1,), (1,)), ((), ()))


def dot(a, b, dims=(((1,), (0,)), ((), ()))):
    return lax.dot_general(a, b, dims, preferred_element_type=jnp.float32)


def feature_map(value):
    return jnp.where(value > 0, value + 1.0, jnp.exp(jnp.minimum(value, 0.0)))


def same_head():
    row = lax.broadcasted_iota(jnp.int32, (D, D), 0) // DH
    col = lax.broadcasted_iota(jnp.int32, (D, D), 1) // DH
    return row == col


def alive_of(count_ref, rows):
    return (lax.broadcasted_iota(jnp.int32, (rows, 1), 0) < count_ref[...]).astype(jnp.float32)


def store_packed(out_ref, dense, vectors):
    kept = jnp.where(same_head(), dense, 0.0)
    folded = kept[0:DH]
    for h in range(1, HEADS):
        folded = folded + kept[h * DH : (h + 1) * DH]
    row = lax.broadcasted_iota(jnp.int32, (TILE, D), 0)
    last = jnp.zeros((TILE, D), jnp.float32)
    for i, vector in enumerate(vectors):
        last = jnp.where(row == i, vector, last)
    tiles = [folded[t * TILE : (t + 1) * TILE] for t in range(4)] + [last]
    for t, tile in enumerate(tiles):
        for r in range(TILE):
            out_ref[r, :, t * D : (t + 1) * D] = tile[r : r + 1]


def load_packed(packed_ref):
    tiles = [
        jnp.concatenate([packed_ref[r, :, t * D : (t + 1) * D] for r in range(TILE)], axis=0) for t in range(5)
    ]
    folded = jnp.concatenate(tiles[:4], axis=0)
    return jnp.where(same_head(), jnp.concatenate([folded] * HEADS, axis=0), 0.0), tiles[4]


def halves(value):
    high = value.astype(jnp.bfloat16)
    return high, (value - high.astype(jnp.float32)).astype(jnp.bfloat16)


def dot3(a, b, dims=(((1,), (0,)), ((), ()))):
    return dot(a[0], b[0], dims) + (dot(a[0], b[1], dims) + dot(a[1], b[0], dims))


def head_sums(value, heads):
    high, low = halves(value)
    return dot(high, heads) + dot(low, heads)


def key_kernel(
    count_ref, feats_hbm, w_hbm, send_hbm, packed_ref, first_ref, second_ref,
    feats_ref, w_ref, send_ref, sems,
):
    sources = [(feats_hbm, feats_ref), (w_hbm.at[pl.ds(1, 2)], w_ref), (send_hbm, send_ref)]
    copies = [pltpu.make_async_copy(*pair, sems.at[i]) for i, pair in enumerate(sources)]
    for copy in copies:
        copy.start()
    for copy in copies:
        copy.wait()
    feats = feats_ref[...]
    slot = lax.broadcasted_iota(jnp.int32, (feats.shape[0], send_ref.shape[2]), 0)
    odd = lax.axis_index("z") % 2
    for turn, out in ((0, first_ref), (1, second_ref)):
        to_after = send_ref[0, 1:2, :] * (1 - odd) + send_ref[0, 0:1, :] * odd
        to_before = send_ref[0, 0:1, :] * (1 - odd) + send_ref[0, 1:2, :] * odd
        chosen = (slot == (to_before if turn else to_after)).astype(jnp.bfloat16)
        out[...] = dot(chosen, feats, ROWS_FIRST).astype(jnp.bfloat16)
    key_map = feature_map(dot(feats, w_ref[0]))
    value_rows = dot(feats, w_ref[1])
    key_map = key_map * alive_of(count_ref, feats.shape[0])
    kv = dot3(halves(key_map), halves(value_rows), ROWS_FIRST)
    live = jnp.broadcast_to(count_ref[...].astype(jnp.float32), (1, D))
    store_packed(packed_ref, kv, [jnp.sum(key_map, axis=0, keepdims=True), live])


def count_hits(nbr_ref, count_ref, hits_ref):
    wide, total = hits_ref.shape
    slots = nbr_ref.shape[0]
    sub = 32
    one, none = jnp.ones((sub, 128), jnp.bfloat16), jnp.zeros((sub, 128), jnp.bfloat16)
    for b in range(total // 128):
        at = slice(b * 128, (b + 1) * 128)
        slot = lax.broadcasted_iota(jnp.int32, (slots, 128), 0)
        named = jnp.where(slot < count_ref[:, at], nbr_ref[:, at], -1)
        rows = [jnp.broadcast_to(named[s : s + 1], (sub, 128)).astype(jnp.int16) for s in range(slots)]
        own = (lax.broadcasted_iota(jnp.int32, (sub, 128), 1) + b * 128).astype(jnp.int16)
        place0 = lax.broadcasted_iota(jnp.int32, (sub, 128), 0)

        def body(i, carry):
            first = pl.multiple_of(i * sub, sub)
            place = (place0 + first).astype(jnp.int16)
            hits = jnp.where(place == own, one, none)
            for s in range(slots):
                hits = hits + jnp.where(place == rows[s], one, none)
            hits_ref[pl.ds(first, sub), at] = hits
            return carry

        lax.fori_loop(0, wide // sub, body, 0)


def graph_kernel(
    nbr_ref, count_ref, feats_ref, first_ref, second_ref, grad_ref, gain_ref, held_ref, gain_out_ref, hits_ref
):
    count_hits(nbr_ref, count_ref, hits_ref)
    total = feats_ref.shape[0]
    rim = first_ref.shape[0]
    odd = lax.axis_index("z") % 2 == 1
    left = jnp.where(odd, first_ref[...], second_ref[...])
    right = jnp.where(odd, second_ref[...], first_ref[...])
    summed = dot(hits_ref[:total, :], feats_ref[...], ROWS_FIRST)
    summed += dot(hits_ref[total : total + rim, :], left, ROWS_FIRST)
    summed += dot(hits_ref[total + rim :, :], right, ROWS_FIRST)
    named = dot(hits_ref[...], jnp.ones((total + 2 * rim, 128), jnp.bfloat16), ROWS_FIRST)
    agg = (summed / jnp.concatenate([named, named], axis=1)).astype(jnp.bfloat16)
    held_ref[0] = agg
    held_ref[1] = grad_ref[...]
    gain_out_ref[...] = gain_ref[...]


def mix_kernel(
    count_ref, packed_ref, feats_ref, w_ref, wg_ref, held_ref, gain_ref,
    out_ref, dnum_ref, packed_out_ref, terms_ref, scale_ref,
):
    kv, vectors = load_packed(packed_ref)
    kv = halves(kv)
    ks, live = vectors[0:1], vectors[1:2]
    factor = 1.0 / (DH * live)
    scale_ref[...] = lax.rsqrt(live)
    heads = same_head().astype(jnp.bfloat16)
    gain_alive = gain_ref[...] * alive_of(count_ref, feats_ref.shape[0])

    feats, agg = feats_ref[...], held_ref[0]
    query_map = feature_map(dot(feats, w_ref[0]))
    query_halves = halves(query_map)
    numer = dot(feats, w_ref[2]) + factor * dot3(query_halves, kv)
    denom = 1.0 + factor * head_sums(query_map * ks, heads)
    inverse = 1.0 / denom
    attn = numer * inverse
    mixed = 0.5 * attn + 0.5 * dot(agg, wg_ref[...])
    mean = jnp.sum(mixed, -1, keepdims=True) / D
    spread = jnp.sum(mixed * mixed, -1, keepdims=True) / D - mean * mean
    rstd = lax.rsqrt(spread + 1e-05)
    normed = (mixed - mean) * rstd
    out_ref[...] = (normed * gain_alive).astype(jnp.bfloat16)
    dnormed = held_ref[1].astype(jnp.float32) * gain_alive
    dmixed = rstd * (
        dnormed
        - jnp.sum(dnormed, -1, keepdims=True) / D
        - normed * (jnp.sum(dnormed * normed, -1, keepdims=True) / D)
    )
    dattn = 0.5 * dmixed
    dnum = dattn * inverse
    dnum_ref[...] = dnum
    dden = -head_sums(dattn * attn, heads) * inverse
    dkv = dot3(query_halves, halves(dnum), ROWS_FIRST)
    dks = jnp.sum(query_map * dden, axis=0, keepdims=True)
    store_packed(packed_out_ref, factor * dkv, [factor * dks])
    terms_ref[0] = dot(agg, dattn.astype(jnp.bfloat16), ROWS_FIRST)
    dquery = factor * (dot3(halves(dnum), kv, COLS_LAST) + dden * ks) * jnp.minimum(query_map, 1.0)
    terms_ref[1] = dot(feats, dquery.astype(jnp.bfloat16), ROWS_FIRST)


def grad_kernel(count_ref, packed_ref, feats_ref, w_ref, dnum_ref, early_ref, terms_ref):
    terms_ref[0] = early_ref[0]
    terms_ref[1] = early_ref[1]
    dkv, vectors = load_packed(packed_ref)
    dkv = halves(dkv)
    feats = feats_ref[...]
    alive = alive_of(count_ref, feats.shape[0])
    key_map = feature_map(dot(feats, w_ref[1]))
    slope = jnp.minimum(key_map, 1.0) * alive
    dvalue = dnum_ref[...] + dot3(halves(key_map * alive), dkv)
    dkey = (dot3(halves(dot(feats, w_ref[2])), dkv, COLS_LAST) + vectors[0:1]) * slope
    terms_ref[2] = dot(feats, dkey.astype(jnp.bfloat16), ROWS_FIRST)
    terms_ref[3] = dot(feats, dvalue.astype(jnp.bfloat16), ROWS_FIRST)


def split_kernel(total_ref, qkv_ref, graph_ref, sems):
    copies = [
        pltpu.make_async_copy(total_ref.at[pl.ds(1, 3)], qkv_ref, sems.at[0]),
        pltpu.make_async_copy(total_ref.at[0], graph_ref, sems.at[1]),
    ]
    for copy in copies:
        copy.start()
    for copy in copies:
        copy.wait()


def call(kernel, shapes, *args, away=(), outs_away=False, scratch=(), limit=VMEM_LIMIT):
    near = pl.BlockSpec(memory_space=pltpu.VMEM)
    far = pl.BlockSpec(memory_space=pltpu.MemorySpace.HBM)
    return pl.pallas_call(
        kernel,
        in_specs=[far if i in away else near for i in range(len(args))],
        out_specs=jax.tree.map(lambda one: far if outs_away else near, shapes),
        out_shape=shapes,
        scratch_shapes=scratch,
        cost_estimate=pl.CostEstimate(flops=10**9, bytes_accessed=10**7, transcendentals=0),
        compiler_params=pltpu.CompilerParams(vmem_limit_bytes=limit),
    )(*args)


def scatter_sum(value, axes, count):
    parts = lax.all_to_all(value, axes, 0, 0, tiled=True)
    return jnp.sum(parts.reshape(count, value.shape[0] // count, *value.shape[1:]), axis=0)


def gather(value, axes, count):
    copies = jnp.broadcast_to(value[None], (count, *value.shape)).reshape(count * value.shape[0], *value.shape[1:])
    return lax.all_to_all(copies, axes, 0, 0, tiled=True)


def gather_sum(value, axes, count):
    return jnp.sum(gather(value, axes, count).reshape(count, *value.shape), axis=0)


def sum_terms(terms, sizes, scale):
    plane = ("x", "z")
    spread = sizes["x"] * sizes["z"]
    value = scatter_sum(terms, "c", sizes["c"])
    value = scatter_sum(value, plane, spread)
    value = gather_sum(value, "y", sizes["y"]) * scale
    value = gather(value, plane, spread)
    return gather(value, "c", sizes["c"])


def local(sizes, node_feats, w_qkv, w_graph, ln_gain, out_grad, part_counts, send_rows, neighbours, neighbour_counts):
    rows = node_feats.shape[0]
    rim = send_rows.shape[2]
    near = sizes["x"] * sizes["c"]
    parts = near * sizes["y"] * sizes["z"]
    f32, bf16 = jnp.float32, jnp.bfloat16
    shape = jax.ShapeDtypeStruct
    count = part_counts.reshape(1, 1)
    rows_f32, rows_bf16 = shape((rows, D), f32), shape((rows, D), bf16)
    packed_shape, rim_shape = shape((TILE, 1, PACK), f32), shape((rim, D), bf16)
    together = lax.optimization_barrier

    packed, first, second = call(
        key_kernel, [packed_shape, rim_shape, rim_shape],
        count, node_feats, w_qkv, send_rows, away=(1, 2, 3), limit=None,
        scratch=[
            pltpu.VMEM((rows, D), bf16), pltpu.VMEM((2, D, D), bf16), pltpu.VMEM(send_rows.shape, jnp.int32),
            pltpu.SemaphoreType.DMA((3,)),
        ],
    )

    swap = [(i, i ^ 1) for i in range(parts)]
    cross = [pair for i in range(1, parts - 1, 2) for pair in ((i, i + 1), (i + 1, i))]
    first = lax.ppermute(first, FINE, swap)
    second = lax.ppermute(second, FINE, cross)
    share = scatter_sum(packed, ("x", "c"), near)
    share, named = together((share, neighbours))
    held, gain = call(
        graph_kernel, [shape((2, rows, D), bf16), shape((1, D), f32)],
        named.T, neighbour_counts.reshape(1, rows), node_feats, first, second, out_grad, ln_gain.reshape(1, D),
        scratch=[pltpu.VMEM((rows + 2 * rim, rows), bf16)],
    )
    share = gather_sum(share, "y", sizes["y"])
    share, held, gain = together((share, held, gain))
    share = gather_sum(share, "z", sizes["z"])
    packed = gather(share, ("x", "c"), near)

    node_out, dnum, dpacked, terms, scale = call(
        mix_kernel, [rows_bf16, rows_f32, packed_shape, shape((2, D, D), f32), shape((1, D), f32)],
        count, packed, node_feats, w_qkv, w_graph, held, gain,
    )

    share = scatter_sum(dpacked, ("x", "c"), near)
    share = gather_sum(share, "y", sizes["y"])
    share = gather_sum(share, "z", sizes["z"])
    dpacked = gather(share, ("x", "c"), near)

    terms = call(grad_kernel, shape((4, D, D), f32), count, dpacked, node_feats, w_qkv, dnum, terms)
    total = sum_terms(terms.reshape(4 * D, D), sizes, scale).reshape(4, D, D)
    qkv_grad, graph_grad = call(
        split_kernel, [shape((3, D, D), f32), shape((D, D), f32)], total,
        outs_away=True, scratch=[pltpu.SemaphoreType.DMA((2,))],
    )
    return node_out, qkv_grad, graph_grad


def solution(mesh):
    sizes = dict(zip(FINE, (*MESH_FACTORS[mesh.shape["dom"]], mesh.shape["head"])))
    fine = Mesh(mesh.devices.reshape(tuple(sizes.values())), FINE)
    return jax.shard_map(
        functools.partial(local, sizes),
        mesh=fine,
        in_specs=(
            P(FINE, None), P(), P(), P(), P(FINE, None), P(FINE), P(FINE, None, None), P(FINE, None), P(FINE),
        ),
        out_specs=(P(FINE, None), P(), P()),
        check_vma=False,
    )
```
